512 devices in a mesh: row: 32 (over y_hi, z, core), col: 16 (over x, y_lo).
Axes of the slice: x: 4, y: 8 (y_hi: 2, y_lo: 4; y = y_hi * 4 + y_lo), z: 8, core: 2. Of those that a mesh axis runs over, the one named last changes fastest.
Arguments:
- curve_embed: bfloat16 [32768, 128], P(('row', 'col')), may hold values from -6 to 6
- solution: float32 [32768, 256], P(('row', 'col')), may hold values from -0.125 to 0.125
- targets: bfloat16 [32768, 256], P(('row', 'col')), may hold values from -6 to 6
- lengths: int32 [32768], P(('row', 'col')), may hold values from 1 to 256
- slot_curve: int32 [32768], P(('row', 'col')), may hold values from 0 to 32767, as said below
- epoch_kernel: float32 [256, 256], replicated, as said below
Outputs:
- row_grad: float32 [32768, 128], P(('row', 'col'))
- col_grad: float32 [32768, 128], P(('row', 'col'))
The draws below stay inside these ranges and needn't reach their ends.
Inputs may be any that keep to these rules, and one draw needn't show every extreme that they name: Within each aligned group of 1024 slots, slot_curve is a permutation of that group's own slot numbers. `epoch_kernel`: symmetric positive definite.
All inputs are finite; a program needn't handle non-finite values.
Results may differ from the reference program's by a relative error of at most 0.0036.
Values may be sent and summed in bfloat16 or wider, within the bound.
A program may use at most 64 MiB of HBM per device.

```python
import math
from functools import partial
import jax
import jax.numpy as jnp
from jax import lax

D = 128
E = 256
NCURVES = 32768
GROUP = 1024


def draw_curve_embed(key, part):
    clusters = max(1, min(64, NCURVES // 16))
    base_key = jax.random.fold_in(key, 37)
    subkeys = jax.random.split(base_key, 5)
    member = jax.random.randint(subkeys[0], (NCURVES,), 0, clusters).astype(jnp.int32)
    spread = jax.random.uniform(subkeys[1], (clusters, 1), jnp.float32, 0.8, 1.5)
    jitter = jax.random.uniform(subkeys[2], (clusters, 1), jnp.float32, 0.4, 0.8)
    centre_raw = jax.random.normal(subkeys[3], (clusters, D), jnp.float32)
    noise_raw = jax.random.normal(subkeys[4], (NCURVES, D), jnp.float32)
    centres = centre_raw * spread
    picked = jnp.take(centres, member, axis=0)
    noise_scale = jnp.take(jitter, member, axis=0)
    mixed = picked + noise_scale * noise_raw
    return jnp.clip(mixed, -6.0, 6.0).astype(jnp.bfloat16)


def draw_slot_curve(key, part):
    groups = NCURVES // GROUP
    subkeys = jax.random.split(jax.random.fold_in(key, 11), groups)
    orders = jax.vmap(partial(jax.random.permutation, x=GROUP))(subkeys)
    shifted = orders + (jnp.arange(groups, dtype=jnp.int32) * GROUP)[:, None]
    return shifted.reshape(NCURVES).astype(jnp.int32)


def draw_epoch_kernel(key, part):
    subkey = jax.random.fold_in(key, 23)
    factor = jax.random.normal(subkey, (E, E), jnp.float32)
    factor = factor / math.sqrt(E)
    product = jnp.dot(factor, factor.T, precision=lax.Precision.HIGHEST)
    return (jnp.eye(E, dtype=jnp.float32) + 0.5 * product).astype(jnp.float32)


def plant(array, own_key, smallest, top_value):
    index_at = [jax.random.randint(jax.random.fold_in(own_key, axis), (), 0, length) for axis, length in enumerate(array.shape)]
    widest = array.shape.index(max(array.shape))
    neighbour = index_at[:widest] + [(index_at[widest] + 1) % array.shape[widest]] + index_at[widest + 1:]
    return array.at[tuple(index_at)].set(smallest).at[tuple(neighbour)].set(top_value)


def block_levels(own_key, shape, cuts, smallest, high):
    def one(dim, shards_of):
        steps = jax.random.uniform(jax.random.fold_in(jax.random.fold_in(own_key, 6), dim), (shards_of,), jnp.float32, smallest / len(cuts), high / len(cuts))
        return jnp.repeat(jnp.exp(steps), shape[dim] // shards_of).reshape((-1,) + (1,) * (len(shape) - dim - 1))

    level = one(*cuts[0])
    for cut in cuts[1:]:
        level = level * one(*cut)
    return level


def scatter_about(own_key, shape, scale, most, shards=(), held_as=jnp.bfloat16):
    array = scale * jax.random.normal(own_key, shape, jnp.float32)
    if shards:
        array = array * block_levels(own_key, shape, shards, -0.22, 0.18)
    return jnp.clip(array, -most, most).astype(held_as)


def setup_inputs(seed: int = 0) -> dict:
    splits = jax.random.split(jax.random.key(seed), 7)
    curve_embed = draw_curve_embed(jax.random.fold_in(splits[6], 71), 0)
    solution = scatter_about(splits[1], (NCURVES, E), (NCURVES // 16) ** -0.5, 0.125, ((0, 512),), jnp.float32)
    targets = scatter_about(splits[2], (NCURVES, E), 1.0, 6.0, ((0, 512),))
    lengths = plant(jax.random.randint(splits[3], (NCURVES,), 1, E + 1), jax.random.fold_in(splits[3], 1), 1, E).astype(jnp.int32)
    slot_curve = draw_slot_curve(jax.random.fold_in(splits[6], 71), 0)
    epoch_kernel = draw_epoch_kernel(jax.random.fold_in(splits[6], 71), 0)
    return {"curve_embed": curve_embed, "solution": solution, "targets": targets, "lengths": lengths, "slot_curve": slot_curve, "epoch_kernel": epoch_kernel}


def kernel_rows(left_embed, right_embed):
    left_wide = left_embed.astype(jnp.float32)
    right_wide = right_embed.astype(jnp.float32)
    products = jnp.dot(left_embed, right_embed.T, preferred_element_type=jnp.float32)
    distance = jnp.sum(left_wide * left_wide, axis=1)[:, None] + jnp.sum(right_wide * right_wide, axis=1)[None, :] - 2.0 * products
    return jnp.exp(-distance / D)


def reference(curve_embed, solution, targets, lengths, slot_curve, epoch_kernel):
    fitted = jnp.dot(solution, epoch_kernel, precision=lax.Precision.HIGHEST, preferred_element_type=jnp.float32).astype(jnp.bfloat16)
    blocks = NCURVES // GROUP
    embed_blocks = curve_embed.reshape(blocks, GROUP, D)

    def fit_block(row_embed):
        kernel = kernel_rows(row_embed, curve_embed).astype(jnp.bfloat16)
        return jnp.dot(kernel, fitted, preferred_element_type=jnp.float32)

    fitted_sum = lax.map(fit_block, embed_blocks).reshape(NCURVES, E)
    epochs = jnp.arange(E, dtype=jnp.int32)
    observed = epochs[None, :] < lengths[:, None]
    adjoint = jnp.where(observed, targets.astype(jnp.float32) - fitted_sum, jnp.float32(0.0)).astype(jnp.bfloat16)
    adjoint_blocks = adjoint.reshape(blocks, GROUP, E)
    embed_wide = curve_embed.astype(jnp.float32)

    def grad_block(col_sum, inputs):
        row_embed, adjoint_rows = inputs
        kernel = kernel_rows(row_embed, curve_embed)
        link = jnp.dot(adjoint_rows, fitted.T, preferred_element_type=jnp.float32)
        weight = (link * kernel).astype(jnp.bfloat16)
        row_wide = row_embed.astype(jnp.float32)
        across = jnp.dot(weight, curve_embed, preferred_element_type=jnp.float32) - row_wide * jnp.sum(weight, axis=1, dtype=jnp.float32)[:, None]
        down = jnp.dot(weight.T, row_embed, preferred_element_type=jnp.float32) - embed_wide * jnp.sum(weight, axis=0, dtype=jnp.float32)[:, None]
        return col_sum + down, across

    start_sum = jnp.zeros((NCURVES, D), jnp.float32)
    col_sum, row_parts = lax.scan(grad_block, start_sum, (embed_blocks, adjoint_blocks))
    factor = 2.0 / D
    slot_rows = row_parts.reshape(NCURVES, D) * factor
    row_grad = jnp.zeros((NCURVES, D), jnp.float32).at[slot_curve].set(slot_rows)
    col_grad = col_sum * factor
    return row_grad, col_grad
```

```python
import jax
import jax.numpy as jnp
from jax import lax
from jax.experimental import pallas as pl
from jax.experimental.pallas import tpu as pltpu
from jax.sharding import PartitionSpec as P

MESH = pl.DeviceIdType.MESH
F32, BF16, I32 = jnp.float32, jnp.bfloat16, jnp.int32

OWN = 64
D = 128
E = 256
ROWS = 1024
COLS = 2048
ZREL = (0, 1, -1, 2, -2, 3, -3, 4)
ZSLOT = {z: k for k, z in enumerate(ZREL)}
ZSLOT[-4] = ZSLOT[4]
STEP = 256

NT = (((1,), (1,)), ((), ()))


def place():
    row, col = lax.axis_index("row"), lax.axis_index("col")
    return row // 16, (row // 2) % 8, row % 2, col // 4, col % 4


def at(h, z, c, x, l):
    return (h * 16 + z * 2 + c, x * 4 + l)


def pieces(wide):
    first = wide.astype(BF16).astype(F32)
    second = (wide - first).astype(BF16).astype(F32)
    third = (wide - first - second).astype(BF16).astype(F32)
    return first, second, third


def extended(embed, ones_first):
    wide = embed.astype(F32)
    squares = jnp.sum(wide * wide, axis=1, keepdims=True) * (-1.0 / D)
    a, b, c = pieces(squares)
    lane = lax.broadcasted_iota(I32, wide.shape, 1)
    at_parts = lane - 3 if ones_first else lane
    at_ones = lane if ones_first else lane - 3
    ones = jnp.where((at_ones >= 0) & (at_ones < 3), 1.0, 0.0)
    parts = jnp.where(at_parts == 0, a, jnp.where(at_parts == 1, b, jnp.where(at_parts == 2, c, ones)))
    return parts.astype(BF16)


def kernel(
    embed_ref, solution_ref, targets_ref, lengths_ref, ids_ref, epoch_ref,
    row_out, col_out,
    colb, cola, rowe, rowa, rowt, kst, facc, fitb, fit_x, fit_ys, fit_y,
    adjb, acr, idb, perm, cgf, cgx, cgr, cgs, cgd, rgf, rgb, rgs, rg_x, rg_ys, rg_y,
    ssem, rsem,
):
    h, z, c, x, l = place()
    count = [0]
    sent = []

    def send(src, dst, device):
        i = count[0]
        count[0] += 1
        copy = pltpu.make_async_remote_copy(
            src_ref=src, dst_ref=dst, send_sem=ssem.at[i], recv_sem=rsem.at[i],
            device_id=device, device_id_type=MESH,
        )
        copy.start()
        sent.append(copy)
        return copy

    core_peer = at(h, z, 1 - c, x, l)
    far_peer = at(1 - h, z, c, x, l)
    z_peer = lambda d: at(h, (z + d + 8) % 8, c, x, l)
    x_peer = lambda d: at(h, z, c, (x + d + 4) % 4, l)
    l_peer = lambda d: at(h, z, c, x, (l + d + 4) % 4)

    barrier = pltpu.get_barrier_semaphore()
    peers = [core_peer, far_peer, z_peer(1), z_peer(-1)]
    peers += [x_peer(d) for d in (1, 2, 3)] + [l_peer(d) for d in (1, 2, 3)]
    for peer in peers:
        pl.semaphore_signal(barrier, inc=1, device_id=peer, device_id_type=MESH)

    def block(slot):
        return pl.ds(slot * OWN, OWN)

    fitted = jnp.dot(
        solution_ref[...], epoch_ref[...], precision=lax.Precision.HIGHEST, preferred_element_type=F32
    )
    colb[0:OWN, 0:D] = embed_ref[...]
    colb[0:OWN, D : D + E] = fitted.astype(BF16)
    rowe[0:OWN, :] = embed_ref[...]
    ids = ids_ref[...]
    idb[0] = jnp.broadcast_to(jnp.concatenate([ids, ids], axis=1), (8, 128))
    pl.semaphore_wait(barrier, len(peers))

    def slot_of(far, zrel, other):
        return far * 16 + ZSLOT[zrel] * 2 + other

    came = {}

    def pass_on(far, zrel):
        src = colb.at[block(slot_of(far, zrel, 0)), :]
        most_up, most_down = (4, 3) if far == 0 else (3, 4)
        if zrel <= 0 and -zrel < most_up:
            came[far, zrel - 1] = send(src, colb.at[block(slot_of(far, zrel - 1, 0)), :], z_peer(1))
        if 0 <= zrel < most_down:
            came[far, zrel + 1] = send(src, colb.at[block(slot_of(far, zrel + 1, 0)), :], z_peer(-1))
        came[far, zrel, "core"] = send(src, colb.at[block(slot_of(far, zrel, 1)), :], core_peer)

    far_copy = send(colb.at[block(0), :], colb.at[block(16), :], far_peer)
    pass_on(0, 0)

    def gather_rows(ref):
        along_l = [send(ref(0), ref(d), l_peer(-d)) for d in (1, 2, 3)]
        along_x = [send(ref(0), ref(d * 4), x_peer(-d)) for d in (1, 2, 3)]

        def spread():
            for d, copy in zip((1, 2, 3), along_l):
                copy.wait_recv()
                along_x.extend(send(ref(d), ref(e * 4 + d), x_peer(-e)) for e in (1, 2, 3))

        def finish():
            for copy in along_x:
                copy.wait_recv()

        return spread, finish

    spread_rows, finish_rows = gather_rows(lambda s: rowe.at[block(s), :])
    spread_ids, finish_ids = gather_rows(lambda s: idb.at[s])

    def arrive(far, zrel):
        came[far, zrel].wait_recv()
        pass_on(far, zrel)

    arrive(0, -1), arrive(0, 1)
    spread_rows()
    arrive(0, -2), arrive(0, 2)
    far_copy.wait_recv()
    pass_on(1, 0)
    arrive(0, -3), arrive(0, 3)
    arrive(0, -4)
    spread_ids()
    finish_rows()

    rowe_all = rowe[...]
    rowa[:, 0:D] = (rowe_all.astype(F32) * (1.0 / 64)).astype(BF16)
    rowa[:, D:] = extended(rowe_all, True)

    arrive(1, -1), arrive(1, 1)
    arrive(1, -2), arrive(1, 2)
    arrive(1, -3), arrive(1, 3)
    arrive(1, 4)
    for far in (0, 1):
        for zrel in ZREL:
            key = (far, -4, "core") if (far == 0 and zrel == 4) else (far, zrel, "core")
            came[key].wait_recv()

    @pl.loop(0, COLS // STEP)
    def _(i):
        rows = pl.ds(i * STEP, STEP)
        embed = colb[rows, 0:D]
        cola[rows, 0:D] = embed
        cola[rows, D:] = extended(embed, False)

    def fit_rows(chunk):
        rows = pl.ds(chunk * STEP, STEP)
        facc[...] = jnp.zeros_like(facc)

        @pl.loop(0, COLS // STEP)
        def _(i):
            cols = pl.ds(i * STEP, STEP)
            power = lax.dot_general(rowa[rows, :], cola[cols, :], NT, preferred_element_type=F32)
            kern = jnp.exp(power)
            kst[i, rows, :] = kern
            facc[...] += jnp.dot(kern.astype(BF16), colb[cols, D : D + E], preferred_element_type=F32)

    fit_copies = {}
    for d in (2, 1, 3):
        fit_rows(d)
        fitb[pl.ds((d - 1) * STEP, STEP), :] = facc[...].astype(BF16)
        fit_copies[d] = send(fitb.at[pl.ds((d - 1) * STEP, STEP), :], fit_x.at[d - 1], x_peer(d))
    fit_rows(0)
    for d in (2, 1, 3):
        fit_copies[d].wait_recv()
        facc[...] += fit_x[d - 1].astype(F32)
    y_copies = []
    for d in (1, 2, 3):
        fit_ys[d - 1] = facc[pl.ds(d * OWN, OWN), :].astype(BF16)
        y_copies.append(send(fit_ys.at[d - 1], fit_y.at[d - 1], l_peer(d)))

    rowt[...] = rowa[...].T
    finish_ids()
    lane = lax.broadcasted_iota(I32, (1, 128), 1)

    @pl.loop(0, 8)
    def _(i):
        both = jnp.where(lane < OWN, idb[2 * i, 0:1, :], idb[2 * i + 1, 0:1, :])
        across_x = (((both >> 8) & 3) - x) & 3
        across_l = (((both >> 6) & 3) - l) & 3
        goal = across_x * 256 + across_l * OWN + (both & (OWN - 1))
        seat = lax.broadcasted_iota(I32, (ROWS, 128), 0)
        perm[i] = jnp.where(seat == goal, 1.0, 0.0).astype(BF16)

    diagonal = lax.broadcasted_iota(I32, (OWN, OWN), 0) == lax.broadcasted_iota(I32, (OWN, OWN), 1)
    spans = jnp.broadcast_to(lengths_ref[...].astype(F32), (OWN, OWN))
    span = jnp.sum(jnp.where(diagonal, spans, 0.0), axis=1, keepdims=True)
    epoch = lax.broadcasted_iota(I32, (OWN, E), 1).astype(F32)

    total = facc[0:OWN, :]
    for d in (1, 2, 3):
        y_copies[d - 1].wait_recv()
        total += fit_y[d - 1].astype(F32)
    adjoint = jnp.where(epoch < span, targets_ref[...].astype(F32) - total, 0.0).astype(BF16)
    adjb[0:OWN, :] = adjoint
    spread_adjoint, finish_adjoint = gather_rows(lambda s: adjb.at[block(s), :])
    spread_adjoint()
    acr[...] = jnp.zeros_like(acr)
    finish_adjoint()

    @pl.loop(0, COLS // STEP)
    def _(i):
        cols = pl.ds(i * STEP, STEP)
        down = jnp.zeros((2 * D, STEP), F32)
        for r in range(ROWS // STEP):
            rows = slice(r * STEP, (r + 1) * STEP)
            link = lax.dot_general(adjb[rows, :], colb[cols, D : D + E], NT, preferred_element_type=F32)
            weight = (link * kst[i, rows, :]).astype(BF16)
            acr[rows, :] += jnp.dot(weight, cola[cols, :], preferred_element_type=F32)
            down += jnp.dot(rowt[:, rows], weight, preferred_element_type=F32)
        turned = down.T
        grad = turned[:, 0:D] * 64.0 - cola[cols, 0:D].astype(F32) * turned[:, D : D + 1]
        for s in range(2):
            mine = grad[2 * s * OWN : (2 * s + 1) * OWN]
            other = grad[(2 * s + 1) * OWN : (2 * s + 2) * OWN]
            cgf[2 * i + s] = mine
            cgx[2 * i + s] = other.astype(BF16)

    core_copy = send(cgx, cgr, core_peer)

    sums = acr[:, D + 3 : D + 4]
    rgb[...] = (acr[:, 0:D] - rowe[...].astype(F32) * sums).astype(BF16)
    placed = jnp.zeros((ROWS, D), F32)
    for i in range(8):
        placed += jnp.dot(perm[i], rgb[i * 128 : (i + 1) * 128, :], preferred_element_type=F32)
    rgf[...] = placed[0:STEP]
    rgs[...] = placed[STEP:].astype(BF16)
    rg_copies = {}
    for d in (2, 1, 3):
        rg_copies[d] = send(rgs.at[pl.ds((d - 1) * STEP, STEP), :], rg_x.at[d - 1], x_peer(d))

    core_copy.wait_recv()
    col_copies = []
    for k in (7, 15, 13, 14, 11, 12, 9, 10, 5, 6, 3, 4, 1, 2, 8):
        far, zrel = k // 8, ZREL[k % 8]
        cgs[k] = (cgf[k] + cgr[k].astype(F32)).astype(BF16)
        owner = at((h + far) % 2, (z + zrel + 8) % 8, c, x, l)
        col_copies.append((k, send(cgs.at[k], cgd.at[k], owner)))

    for d in (2, 1, 3):
        rg_copies[d].wait_recv()
        rgf[...] += rg_x[d - 1].astype(F32)
    last = []
    for d in (1, 2, 3):
        rg_ys[d - 1] = rgf[pl.ds(d * OWN, OWN), :].astype(BF16)
        last.append(send(rg_ys.at[d - 1], rg_y.at[d - 1], l_peer(d)))
    row_total = rgf[0:OWN, :]
    for d in (1, 2, 3):
        last[d - 1].wait_recv()
        row_total += rg_y[d - 1].astype(F32)
    row_out[...] = row_total * (2.0 / D)

    col_total = cgf[0] + cgr[0].astype(F32)
    for k, copy in col_copies:
        copy.wait_recv()
        col_total += cgd[k].astype(F32)
    col_out[...] = col_total * (2.0 / D)
    for copy in sent:
        copy.wait_send()


def per_device(curve_embed, solution, targets, lengths, slot_curve, epoch_kernel):
    vmem = pl.BlockSpec(memory_space=pltpu.VMEM)
    scratch = [
        ((COLS, D + E), BF16), ((COLS, 2 * D), BF16), ((ROWS, D), BF16), ((ROWS, 2 * D), BF16),
        ((2 * D, ROWS), BF16), ((COLS // STEP, ROWS, STEP), F32), ((STEP, E), F32), ((3 * STEP, E), BF16),
        ((3, STEP, E), BF16), ((3, OWN, E), BF16), ((3, OWN, E), BF16),
        ((ROWS, E), BF16), ((ROWS, 2 * D), F32), ((16, 8, 128), I32), ((8, ROWS, 128), BF16),
        ((16, OWN, D), F32), ((16, OWN, D), BF16), ((16, OWN, D), BF16), ((16, OWN, D), BF16),
        ((16, OWN, D), BF16), ((STEP, D), F32), ((ROWS, D), BF16), ((3 * STEP, D), BF16),
        ((3, STEP, D), BF16), ((3, OWN, D), BF16), ((3, OWN, D), BF16),
    ]
    return pl.pallas_call(
        kernel,
        out_shape=(jax.ShapeDtypeStruct((OWN, D), F32), jax.ShapeDtypeStruct((OWN, D), F32)),
        in_specs=[vmem] * 6,
        out_specs=(vmem, vmem),
        scratch_shapes=[pltpu.VMEM(s, t) for s, t in scratch]
        + [pltpu.SemaphoreType.DMA((128,)), pltpu.SemaphoreType.DMA((128,))],
        compiler_params=pltpu.CompilerParams(
            collective_id=0, has_side_effects=True, vmem_limit_bytes=56 * 2**20
        ),
        name="tile",
    )(curve_embed, solution, targets, lengths.reshape(1, OWN), slot_curve.reshape(1, OWN), epoch_kernel)


def solution(mesh):
    both = ("row", "col")
    return jax.shard_map(
        per_device,
        mesh=mesh,
        in_specs=(P(both, None), P(both, None), P(both, None), P(both), P(both), P()),
        out_specs=(P(both, None), P(both, None)),
        check_vma=False,
    )
```

```python
import jax
import jax.numpy as jnp
from jax import lax
from jax.experimental import pallas as pl
from jax.experimental.pallas import tpu as pltpu
from jax.sharding import PartitionSpec as P

MESH = pl.DeviceIdType.MESH
F32, BF16, I32 = jnp.float32, jnp.bfloat16, jnp.int32

OWN = 64
D = 128
E = 256
ROWS = 1024
COLS = 2048
ZREL = (0, 1, -1, 2, -2, 3, -3, 4)
ZSLOT = {z: k for k, z in enumerate(ZREL)}
ZSLOT[-4] = ZSLOT[4]
STEP = 256
TURNED = 144

NT = (((1,), (1,)), ((), ()))


def place():
    row, col = lax.axis_index("row"), lax.axis_index("col")
    return row // 16, (row // 2) % 8, row % 2, col // 4, col % 4


def at(h, z, c, x, l):
    return (h * 16 + z * 2 + c, x * 4 + l)


def pieces(wide):
    first = wide.astype(BF16).astype(F32)
    second = (wide - first).astype(BF16).astype(F32)
    third = (wide - first - second).astype(BF16).astype(F32)
    return first, second, third


def extended(embed, ones_first):
    wide = embed.astype(F32)
    squares = jnp.sum(wide * wide, axis=1, keepdims=True) * (-1.0 / D)
    a, b, c = pieces(squares)
    lane = lax.broadcasted_iota(I32, wide.shape, 1)
    at_parts = lane - 3 if ones_first else lane
    at_ones = lane if ones_first else lane - 3
    ones = jnp.where((at_ones >= 0) & (at_ones < 3), 1.0, 0.0)
    parts = jnp.where(at_parts == 0, a, jnp.where(at_parts == 1, b, jnp.where(at_parts == 2, c, ones)))
    return parts.astype(BF16)


def kernel(
    embed_hbm, solution_hbm, targets_hbm, lengths_hbm, ids_hbm, epoch_hbm,
    row_out, col_out,
    embed_ref, solution_ref, targets_ref, lengths_ref, ids_ref, epoch_ref,
    colb, cola, colt, rowe, rowa, rowt, kst, facc, fitb, fit_x, fit_s, fit_y,
    adjb, acr, idb, perm, dnt, gtb, cgf, cgx, cgr, cgs, cgd, rgb, rgf, rgs, rg_x, rg_s, rg_y,
    ssem, rsem, lsem,
):
    h, z, c, x, l = place()
    count = [0]
    sent = []

    def send(src, dst, device):
        i = count[0]
        count[0] += 1
        copy = pltpu.make_async_remote_copy(
            src_ref=src, dst_ref=dst, send_sem=ssem.at[i], recv_sem=rsem.at[i],
            device_id=device, device_id_type=MESH,
        )
        copy.start()
        sent.append(copy)
        return copy

    core_peer = at(h, z, 1 - c, x, l)
    far_peer = at(1 - h, z, c, x, l)
    z_peer = lambda d: at(h, (z + d + 8) % 8, c, x, l)
    plane_peer = lambda dx, dl: at(h, z, c, (x + dx + 4) % 4, (l + dl + 4) % 4)

    barrier = pltpu.get_barrier_semaphore()
    peers = [core_peer, far_peer] + [z_peer(d) for d in (1, -1, 2, -2)]
    peers += [plane_peer(d, 0) for d in (1, 2, 3)] + [plane_peer(0, d) for d in (1, 2, 3)]
    for peer in peers:
        pl.semaphore_signal(barrier, inc=1, device_id=peer, device_id_type=MESH)

    loads = [
        pltpu.make_async_copy(src, dst, lsem.at[i])
        for i, (src, dst) in enumerate([
            (solution_hbm, solution_ref), (epoch_hbm, epoch_ref), (embed_hbm, embed_ref),
            (ids_hbm, ids_ref), (targets_hbm, targets_ref), (lengths_hbm, lengths_ref),
        ])
    ]
    for load in loads:
        load.start()
    for load in loads[:4]:
        load.wait()

    def block(slot):
        return pl.ds(slot * OWN, OWN)

    fitted = jnp.dot(
        solution_ref[...], epoch_ref[...], precision=lax.Precision.HIGHEST, preferred_element_type=F32
    )
    colb[0:OWN, 0:D] = embed_ref[...]
    colb[0:OWN, D : D + E] = fitted.astype(BF16)
    rowe[0:OWN, :] = embed_ref[...]
    ids = ids_ref[...]
    idb[0] = jnp.broadcast_to(jnp.concatenate([ids, ids], axis=1), (8, 128))
    pl.semaphore_wait(barrier, len(peers))

    def slot_of(far, zrel, other):
        return far * 16 + ZSLOT[zrel] * 2 + other

    came = {}

    def forward(far, zrel, steps):
        for step in steps:
            goal = zrel - step
            came[far, ZSLOT[goal]] = send(
                colb.at[block(slot_of(far, zrel, 0)), :], colb.at[block(slot_of(far, goal, 0)), :], z_peer(step)
            )

    def share(far, zrel):
        came[far, ZSLOT[zrel], "core"] = send(
            colb.at[block(slot_of(far, zrel, 0)), :], colb.at[block(slot_of(far, zrel, 1)), :], core_peer
        )

    def arrive(far, zrel):
        came[far, ZSLOT[zrel]].wait_recv()
        share(far, zrel)

    far_copy = send(colb.at[block(0), :], colb.at[block(16), :], far_peer)
    forward(0, 0, (1, -1, 2, -2))
    share(0, 0)

    def gather_rows(ref):
        along_l = [send(ref(0), ref(d), plane_peer(0, -d)) for d in (1, 2, 3)]
        along_x = [send(ref(0), ref(d * 4), plane_peer(-d, 0)) for d in (2, 1, 3)]

        def spread():
            for d, copy in zip((1, 2, 3), along_l):
                copy.wait_recv()
                along_x.extend(send(ref(d), ref(e * 4 + d), plane_peer(-e, 0)) for e in (2, 1, 3))

        def finish():
            for copy in along_x:
                copy.wait_recv()

        return spread, finish

    spread_rows, finish_rows = gather_rows(lambda s: rowe.at[block(s), :])

    arrive(0, -1), arrive(0, 1)
    arrive(0, -2)
    forward(0, -2, (2, 1))
    arrive(0, 2)
    forward(0, 2, (-1,))
    far_copy.wait_recv()
    forward(1, 0, (-2, 2, -1, 1))
    share(1, 0)
    spread_rows()
    arrive(0, -3), arrive(0, 3), arrive(0, 4)
    arrive(1, 2)
    forward(1, 2, (-2, -1))
    arrive(1, -2)
    forward(1, -2, (1,))
    arrive(1, -1), arrive(1, 1)

    finish_rows()
    id_copies = [send(idb.at[0], idb.at[s], plane_peer(-(s // 4), -(s % 4))) for s in range(1, 16)]
    rowe_all = rowe[...]
    rowa[:, 0:D] = (rowe_all.astype(F32) * (1.0 / 64)).astype(BF16)
    rowa[:, D:] = extended(rowe_all, True)

    def columns_in(far):
        for k in range(8):
            came[far, k, "core"].wait_recv()
        cols = slice(far * COLS // 2, (far + 1) * COLS // 2)
        embed = colb[cols, 0:D]
        cola[cols, 0:D] = embed
        cola[cols, D:] = extended(embed, False)

    def fit_rows(far, rows, total):
        for i in range(far * 4, far * 4 + 4):
            cols = slice(i * STEP, (i + 1) * STEP)
            power = lax.dot_general(rowa[rows, :], cola[cols, :], NT, preferred_element_type=F32)
            kern = jnp.exp(power)
            kst[i, rows, :] = kern
            part = jnp.dot(kern.astype(BF16), colb[cols, D : D + E], preferred_element_type=F32)
            total = part if total is None else total + part
        return total

    columns_in(0)

    @pl.loop(0, ROWS // STEP)
    def _(r):
        rows = pl.ds(r * STEP, STEP)
        facc[rows, :] = fit_rows(0, rows, None)

    arrive(1, -3), arrive(1, 3), arrive(1, 4)
    columns_in(1)

    def scatter(d, ref, got):
        return {r: send(ref.at[block(4 * d + r), :], got.at[4 * (d - 1) + r], plane_peer(d, 0)) for r in (2, 1, 3, 0)}

    def reduce_rows(copies, mine, got, going, ends):
        last = []
        for r in (2, 1, 3, 0):
            for d in (2, 1, 3):
                copies[d][r].wait_recv()
            rows = block(r)
            mine[rows, :] += sum(got[4 * d + r].astype(F32) for d in range(3))
            if r:
                going[r - 1] = mine[rows, :].astype(BF16)
                last.append(send(going.at[r - 1], ends.at[r - 1], plane_peer(0, r)))
        return last

    fit_copies = {}
    for d in (2, 1, 3, 0):
        rows = slice(d * STEP, (d + 1) * STEP)
        total = fit_rows(1, rows, facc[rows, :])
        if d:
            fitb[rows, :] = total.astype(BF16)
            fit_copies[d] = scatter(d, fitb, fit_x)
        else:
            facc[rows, :] = total

    fit_last = reduce_rows(fit_copies, facc, fit_x, fit_s, fit_y)

    rowt[...] = rowa[...].T[0:TURNED]
    colt[...] = colb[:, 0:D].T
    acr[...] = jnp.zeros_like(acr)
    for copy in id_copies:
        copy.wait_recv()
    lane = lax.broadcasted_iota(I32, (1, 128), 1)

    @pl.loop(0, 8)
    def _(i):
        both = jnp.where(lane < OWN, idb[2 * i, 0:1, :], idb[2 * i + 1, 0:1, :])
        across_x = (((both >> 8) & 3) - x) & 3
        across_l = (((both >> 6) & 3) - l) & 3
        goal = across_x * 256 + across_l * OWN + (both & (OWN - 1))
        seat = lax.broadcasted_iota(I32, (ROWS, 128), 0)
        perm[i // 2, :, pl.ds(pl.multiple_of((i % 2) * 128, 128), 128)] = jnp.where(seat == goal, 1.0, 0.0).astype(BF16)

    for load in loads[4:]:
        load.wait()
    diagonal = lax.broadcasted_iota(I32, (OWN, OWN), 0) == lax.broadcasted_iota(I32, (OWN, OWN), 1)
    spans = jnp.broadcast_to(lengths_ref[...].astype(F32), (OWN, OWN))
    span = jnp.sum(jnp.where(diagonal, spans, 0.0), axis=1, keepdims=True)
    epoch = lax.broadcasted_iota(I32, (OWN, E), 1).astype(F32)

    total = facc[0:OWN, :]
    for r, copy in enumerate(fit_last):
        copy.wait_recv()
    total += sum(fit_y[r].astype(F32) for r in range(3))
    adjoint = jnp.where(epoch < span, targets_ref[...].astype(F32) - total, 0.0).astype(BF16)
    adjb[0:OWN, :] = adjoint
    spread_adjoint, finish_adjoint = gather_rows(lambda s: adjb.at[block(s), :])
    spread_adjoint()

    def grad_rows(i, rows):
        cols = pl.ds(i * STEP, STEP)
        link = lax.dot_general(adjb[rows, :], colb[cols, D : D + E], NT, preferred_element_type=F32)
        weight = (link * kst[i, rows, :]).astype(BF16)
        acr[rows, :] += jnp.dot(weight, cola[cols, :], preferred_element_type=F32)
        return jnp.dot(rowt[:, rows], weight, preferred_element_type=F32)

    @pl.loop(0, COLS // STEP, step=2)
    def _(i):
        for j in (i, i + 1):
            dnt[j] = grad_rows(j, slice(0, STEP))

    finish_adjoint()

    col_copies = []
    swaps = {}

    def add_cores(i):
        swaps[i].wait_recv()
        for k in (2 * i + 1, 2 * i):
            if k == 0:
                continue
            far, zrel = k // 8, ZREL[k % 8]
            cgs[k] = (cgf[k] + cgr[k].astype(F32)).astype(BF16)
            owner = at((h + far) % 2, (z + zrel + 8) % 8, c, x, l)
            col_copies.append((k, send(cgs.at[k], cgd.at[k], owner)))

    def turn(i, n):
        turned = gtb[n % 2].T
        for s in range(2):
            cgf[2 * i + s] = turned[2 * s * OWN : (2 * s + 1) * OWN]
            cgx[2 * i + s] = turned[(2 * s + 1) * OWN : (2 * s + 2) * OWN].astype(BF16)

    def swap(i):
        pair = pl.ds(2 * i, 2)
        swaps[i] = send(cgx.at[pair], cgr.at[pair], core_peer)

    order = (7, 6, 5, 3, 4, 2, 1, 0)
    for n, i in enumerate(order):
        down = dnt[i] + grad_rows(i, slice(STEP, ROWS))
        gtb[n % 2] = down[0:D] * 64.0 - colt[:, i * STEP : (i + 1) * STEP].astype(F32) * down[D : D + 1]
        if n:
            turn(order[n - 1], n - 1)
            swap(order[n - 1])
        if n > 1:
            add_cores(order[n - 2])
    turn(0, 7)
    swap(0)

    sums = acr[:, D + 3 : D + 4]
    rgb[...] = (acr[:, 0:D] - rowe[...].astype(F32) * sums).astype(BF16)

    def placed(d):
        rows = slice(d * STEP, (d + 1) * STEP)
        return sum(
            jnp.dot(perm[i, rows, :], rgb[i * STEP : (i + 1) * STEP, :], preferred_element_type=F32) for i in range(4)
        )

    row_copies = {}
    for d in (2, 1, 3):
        rgs[d * STEP : (d + 1) * STEP, :] = placed(d).astype(BF16)
        row_copies[d] = scatter(d, rgs, rg_x)
    rgf[...] = placed(0)
    add_cores(order[-2])
    add_cores(order[-1])

    row_last = reduce_rows(row_copies, rgf, rg_x, rg_s, rg_y)
    for copy in row_last:
        copy.wait_recv()
    row_total = rgf[0:OWN, :] + sum(rg_y[r].astype(F32) for r in range(3))
    row_out[...] = row_total * (2.0 / D)

    for k, copy in col_copies:
        copy.wait_recv()
    col_total = cgf[0] + cgr[0].astype(F32)
    for k, copy in col_copies:
        col_total += cgd[k].astype(F32)
    col_out[...] = col_total * (2.0 / D)
    for copy in sent:
        copy.wait_send()


def per_device(curve_embed, solution, targets, lengths, slot_curve, epoch_kernel):
    vmem = pl.BlockSpec(memory_space=pltpu.VMEM)
    scratch = [
        ((OWN, D), BF16), ((OWN, E), F32), ((OWN, E), BF16), ((1, OWN), I32), ((1, OWN), I32), ((E, E), F32),
        ((COLS, D + E), BF16), ((COLS, 2 * D), BF16), ((D, COLS), BF16), ((ROWS, D), BF16), ((ROWS, 2 * D), BF16),
        ((TURNED, ROWS), BF16), ((COLS // STEP, ROWS, STEP), F32), ((ROWS, E), F32), ((ROWS, E), BF16),
        ((12, OWN, E), BF16), ((3, OWN, E), BF16), ((3, OWN, E), BF16),
        ((ROWS, E), BF16), ((ROWS, 2 * D), F32), ((16, 8, 128), I32), ((4, ROWS, STEP), BF16),
        ((COLS // STEP, TURNED, STEP), F32), ((2, D, STEP), F32),
        ((16, OWN, D), F32), ((16, OWN, D), BF16), ((16, OWN, D), BF16), ((16, OWN, D), BF16),
        ((16, OWN, D), BF16), ((ROWS, D), BF16), ((STEP, D), F32), ((ROWS, D), BF16),
        ((12, OWN, D), BF16), ((3, OWN, D), BF16), ((3, OWN, D), BF16),
    ]
    return pl.pallas_call(
        kernel,
        out_shape=(jax.ShapeDtypeStruct((OWN, D), F32), jax.ShapeDtypeStruct((OWN, D), F32)),
        in_specs=[pl.BlockSpec(memory_space=pl.ANY)] * 6,
        out_specs=(vmem, vmem),
        scratch_shapes=[pltpu.VMEM(s, t) for s, t in scratch]
        + [pltpu.SemaphoreType.DMA((160,)), pltpu.SemaphoreType.DMA((160,)), pltpu.SemaphoreType.DMA((6,))],
        compiler_params=pltpu.CompilerParams(
            collective_id=0, has_side_effects=True, vmem_limit_bytes=56 * 2**20
        ),
        name="tile",
    )(curve_embed, solution, targets, lengths.reshape(1, OWN), slot_curve.reshape(1, OWN), epoch_kernel)


def solution(mesh):
    both = ("row", "col")
    return jax.shard_map(
        per_device,
        mesh=mesh,
        in_specs=(P(both, None), P(both, None), P(both, None), P(both), P(both), P()),
        out_specs=(P(both, None), P(both, None)),
        check_vma=False,
    )
```

```python
import jax
import jax.numpy as jnp
from jax import lax
from jax.experimental import pallas as pl
from jax.experimental.pallas import tpu as pltpu
from jax.sharding import PartitionSpec as P

MESH = pl.DeviceIdType.MESH
F32, BF16, I32 = jnp.float32, jnp.bfloat16, jnp.int32

OWN = 64
D = 128
E = 256
ROWS = 1024
COLS = 2048
ZREL = (0, 1, -1, 2, -2, 3, -3, 4)
ZSLOT = {z: k for k, z in enumerate(ZREL)}
ZSLOT[-4] = ZSLOT[4]
STEP = 256
EARLY = 6
PART = 512
TURNED = 144

NT = (((1,), (1,)), ((), ()))


def place():
    row, col = lax.axis_index("row"), lax.axis_index("col")
    return row // 16, (row // 2) % 8, row % 2, col // 4, col % 4


def at(h, z, c, x, l):
    return (h * 16 + z * 2 + c, x * 4 + l)


def pieces(wide):
    first = wide.astype(BF16).astype(F32)
    second = (wide - first).astype(BF16).astype(F32)
    third = (wide - first - second).astype(BF16).astype(F32)
    return first, second, third


def extended(embed, ones_first):
    wide = embed.astype(F32)
    squares = jnp.sum(wide * wide, axis=1, keepdims=True) * (-1.0 / D)
    a, b, c = pieces(squares)
    lane = lax.broadcasted_iota(I32, wide.shape, 1)
    at_parts = lane - 3 if ones_first else lane
    at_ones = lane if ones_first else lane - 3
    ones = jnp.where((at_ones >= 0) & (at_ones < 3), 1.0, 0.0)
    parts = jnp.where(at_parts == 0, a, jnp.where(at_parts == 1, b, jnp.where(at_parts == 2, c, ones)))
    return parts.astype(BF16)


def kernel(
    embed_hbm, solution_hbm, targets_hbm, lengths_hbm, ids_hbm, epoch_hbm,
    out,
    embed_ref, solution_ref, targets_ref, lengths_ref, ids_ref, epoch_ref,
    colb, cola, colt, rowe, rowa, rowt, kst, facc, fitb, fit_x, fit_s, fit_y,
    adjb, acr, wgt, idb, perm, dnt, gtb, cgf, cgx, cgr, cgs, cgd, rgb, rgf, rgs, rg_x, rg_s, rg_y,
    ssem, rsem, lsem,
):
    h, z, c, x, l = place()
    count = [0]
    sent = []

    def send(src, dst, device):
        i = count[0]
        count[0] += 1
        copy = pltpu.make_async_remote_copy(
            src_ref=src, dst_ref=dst, send_sem=ssem.at[i], recv_sem=rsem.at[i],
            device_id=device, device_id_type=MESH,
        )
        copy.start()
        sent.append(copy)
        return copy

    core_peer = at(h, z, 1 - c, x, l)
    far_peer = at(1 - h, z, c, x, l)
    z_peer = lambda d: at(h, (z + d + 8) % 8, c, x, l)
    plane_peer = lambda dx, dl: at(h, z, c, (x + dx + 4) % 4, (l + dl + 4) % 4)

    barrier = pltpu.get_barrier_semaphore()
    peers = [core_peer, far_peer] + [z_peer(d) for d in (1, -1, 2, -2)]
    peers += [plane_peer(d, 0) for d in (1, 2, 3)] + [plane_peer(0, d) for d in (1, 2, 3)]
    for peer in peers:
        pl.semaphore_signal(barrier, inc=1, device_id=peer, device_id_type=MESH)

    loads = [
        pltpu.make_async_copy(src, dst, lsem.at[i])
        for i, (src, dst) in enumerate([
            (solution_hbm, solution_ref), (epoch_hbm, epoch_ref), (embed_hbm, embed_ref),
            (ids_hbm, ids_ref), (targets_hbm, targets_ref), (lengths_hbm, lengths_ref),
        ])
    ]
    for load in loads:
        load.start()
    for load in loads[:4]:
        load.wait()

    def block(slot):
        return pl.ds(slot * OWN, OWN)

    fitted = jnp.dot(
        solution_ref[...], epoch_ref[...], precision=lax.Precision.HIGHEST, preferred_element_type=F32
    )
    colb[0:OWN, 0:D] = embed_ref[...]
    colb[0:OWN, D : D + E] = fitted.astype(BF16)
    rowe[0:OWN, :] = embed_ref[...]
    ids = ids_ref[...]
    idb[0] = jnp.broadcast_to(jnp.concatenate([ids, ids], axis=1), (8, 128))
    pl.semaphore_wait(barrier, len(peers))

    def slot_of(far, zrel, other):
        return far * 16 + ZSLOT[zrel] * 2 + other

    came = {}

    def forward(far, zrel, steps):
        for step in steps:
            goal = zrel - step
            came[far, ZSLOT[goal]] = send(
                colb.at[block(slot_of(far, zrel, 0)), :], colb.at[block(slot_of(far, goal, 0)), :], z_peer(step)
            )

    def share(far, zrel):
        came[far, ZSLOT[zrel], "core"] = send(
            colb.at[block(slot_of(far, zrel, 0)), :], colb.at[block(slot_of(far, zrel, 1)), :], core_peer
        )

    def arrive(far, zrel):
        came[far, ZSLOT[zrel]].wait_recv()
        share(far, zrel)

    far_copy = send(colb.at[block(0), :], colb.at[block(16), :], far_peer)
    forward(0, 0, (1, -1, 2, -2))
    share(0, 0)

    def gather_rows(ref):
        along_l = [send(ref(0), ref(d), plane_peer(0, -d)) for d in (1, 2, 3)]
        along_x = {}

        def go(e, d):
            along_x[e, d] = send(ref(d), ref(e * 4 + d), plane_peer(-e, 0))

        for e in (1, 3, 2):
            go(e, 0)

        def spread():
            for d, copy in zip((1, 2, 3), along_l):
                copy.wait_recv()
                go(1, d), go(3, d)
            for d in (1, 2, 3):
                go(2, d)

        def finish(e):
            for d in range(4):
                along_x[e, d].wait_recv()

        return spread, finish

    spread_rows, finish_rows = gather_rows(lambda s: rowe.at[block(s), :])

    arrive(0, -1), arrive(0, 1)
    spread_rows()
    far_copy.wait_recv()
    forward(1, 0, (-2, 2, -1, 1))
    share(1, 0)
    arrive(0, 2), arrive(0, -2)
    forward(0, -2, (2, 1))
    forward(0, 2, (-1,))
    for e in (1, 2, 3):
        finish_rows(e)
    id_copies = [send(idb.at[0], idb.at[s], plane_peer(-(s // 4), -(s % 4))) for s in range(1, 16)]
    rowe_all = rowe[...]
    rowa[:, 0:D] = (rowe_all.astype(F32) * (1.0 / 64)).astype(BF16)
    rowa[:, D:] = extended(rowe_all, True)

    def columns_in(part):
        for k in range(4 * part, 4 * part + 4):
            came[k // 8, k % 8, "core"].wait_recv()
        cols = slice(part * PART, (part + 1) * PART)
        embed = colb[cols, 0:D]
        cola[cols, 0:D] = embed
        cola[cols, D:] = extended(embed, False)

    def kernel_rows(part, r):
        rows = slice(r * STEP, (r + 1) * STEP)
        cols = slice(part * PART, (part + 1) * PART)
        kern = jnp.exp(lax.dot_general(rowa[rows, :], cola[cols, :], NT, preferred_element_type=F32))
        kst[2 * part, rows, :] = kern[:, 0:STEP]
        kst[2 * part + 1, rows, :] = kern[:, STEP:PART]

    def fit_rows(part, r):
        rows = slice(r * STEP, (r + 1) * STEP)
        total = None if part == 0 else facc[rows, :]
        for i in (2 * part, 2 * part + 1):
            field = colb[i * STEP : (i + 1) * STEP, D : D + E]
            one = jnp.dot(kst[i, rows, :].astype(BF16), field, preferred_element_type=F32)
            total = one if total is None else total + one
        facc[rows, :] = total

    def fit_part(part, done=lambda r: None):
        columns_in(part)
        order = (2, 1, 3, 0)
        kernel_rows(part, order[0])
        for n, r in enumerate(order):
            if n < 3:
                kernel_rows(part, order[n + 1])
            fit_rows(part, r)
            done(r)

    fit_part(0)
    arrive(1, 2)
    forward(1, 2, (-2, -1))
    arrive(1, -2)
    forward(1, -2, (1,))
    arrive(1, -1), arrive(1, 1)
    arrive(0, -3), arrive(0, 3), arrive(0, 4)
    fit_part(2)
    fit_part(1)
    arrive(1, -3), arrive(1, 3), arrive(1, 4)

    def scatter(d, ref, got):
        return {r: send(ref.at[block(4 * d + r), :], got.at[4 * (d - 1) + r], plane_peer(d, 0)) for r in (2, 1, 3, 0)}

    def reduce_rows(copies, mine, got, going, ends):
        last = []
        for r in (2, 1, 3, 0):
            for d in (2, 1, 3):
                copies[d][r].wait_recv()
            rows = block(r)
            mine[rows, :] += sum(got[4 * d + r].astype(F32) for d in range(3))
            if r:
                going[r - 1] = mine[rows, :].astype(BF16)
                last.append(send(going.at[r - 1], ends.at[r - 1], plane_peer(0, r)))
        return last

    passing, below, above = {}, {}, {}

    def put(d, r, slot, step):
        return send(fitb.at[block(4 * d + r), :], fit_x.at[slot], plane_peer(step, 0))

    def leave(d):
        if d == 2:
            rows = slice(d * STEP, (d + 1) * STEP)
            fitb[rows, :] = facc[rows, :].astype(BF16)
            for r in (2, 3, 1, 0):
                passing[r] = put(2, r, 8 + r, 1 if r in (1, 2) else -1)
        if d == 1:
            for r in (3, 0):
                fitb[block(4 + r), :] = facc[block(4 + r), :].astype(BF16)
                below[r] = put(1, r, r, 1)
        if d == 3:
            for r in (2, 1):
                fitb[block(12 + r), :] = facc[block(12 + r), :].astype(BF16)
                above[r] = put(3, r, 4 + r, -1)

    fit_part(3, leave)
    for r in (2, 3, 1, 0):
        passing[r].wait_recv()
        d = 1 if r in (1, 2) else 3
        fitb[block(4 * d + r), :] = (facc[block(4 * d + r), :] + fit_x[8 + r].astype(F32)).astype(BF16)
        if d == 1:
            below[r] = put(1, r, r, 1)
        else:
            above[r] = put(3, r, 4 + r, -1)
    fit_last = []
    for r in (2, 3, 1, 0):
        below[r].wait_recv()
        above[r].wait_recv()
        facc[block(r), :] += fit_x[r].astype(F32) + fit_x[4 + r].astype(F32)
        if r:
            fit_s[r - 1] = facc[block(r), :].astype(BF16)
            fit_last.append(send(fit_s.at[r - 1], fit_y.at[r - 1], plane_peer(0, r)))

    rowt[...] = rowa[...].T[0:TURNED]
    colt[...] = colb[:, 0:D].T
    for copy in id_copies:
        copy.wait_recv()
    lane = lax.broadcasted_iota(I32, (1, 128), 1)

    @pl.loop(0, 8)
    def _(i):
        both = jnp.where(lane < OWN, idb[2 * i, 0:1, :], idb[2 * i + 1, 0:1, :])
        across_x = (((both >> 8) & 3) - x) & 3
        across_l = (((both >> 6) & 3) - l) & 3
        goal = across_x * 256 + across_l * OWN + (both & (OWN - 1))
        seat = lax.broadcasted_iota(I32, (ROWS, 128), 0)
        perm[i // 2, :, pl.ds(pl.multiple_of((i % 2) * 128, 128), 128)] = jnp.where(seat == goal, 1.0, 0.0).astype(BF16)

    for load in loads[4:]:
        load.wait()
    diagonal = lax.broadcasted_iota(I32, (OWN, OWN), 0) == lax.broadcasted_iota(I32, (OWN, OWN), 1)
    spans = jnp.broadcast_to(lengths_ref[...].astype(F32), (OWN, OWN))
    span = jnp.sum(jnp.where(diagonal, spans, 0.0), axis=1, keepdims=True)
    epoch = lax.broadcasted_iota(I32, (OWN, E), 1).astype(F32)

    total = facc[0:OWN, :]
    for copy in fit_last:
        copy.wait_recv()
    total += sum(fit_y[r].astype(F32) for r in range(3))
    adjoint = jnp.where(epoch < span, targets_ref[...].astype(F32) - total, 0.0).astype(BF16)
    adjb[0:OWN, :] = adjoint
    spread_adjoint, finish_adjoint = gather_rows(lambda s: adjb.at[block(s), :])
    spread_adjoint()

    def weigh(i, rows):
        cols = slice(i * STEP, (i + 1) * STEP)
        link = lax.dot_general(adjb[rows, :], colb[cols, D : D + E], NT, preferred_element_type=F32)
        wgt[i, rows, :] = (link * kst[i, rows, :]).astype(BF16)

    def across(i, rows):
        part = jnp.dot(wgt[i, rows, :], cola[i * STEP : (i + 1) * STEP, :], preferred_element_type=F32)
        if i == order[0]:
            acr[rows, :] = part
        else:
            acr[rows, :] += part

    def down(i, rows):
        return jnp.dot(rowt[:, rows], wgt[i, rows, :], preferred_element_type=F32)

    order = (7, 6, 5, 4, 3, 2, 1, 0)

    def rows_arrived(e):
        rows = slice(e * STEP, (e + 1) * STEP)
        weigh(order[0], rows)
        for n, i in enumerate(order):
            if n < 7:
                weigh(order[n + 1], rows)
            across(i, rows)
            part = down(i, rows)
            if e == 0:
                dnt[i] = part
            else:
                dnt[i] += part

    rows_arrived(0)
    finish_adjoint(1)
    rows_arrived(1)
    finish_adjoint(3)
    finish_adjoint(2)

    def finish(i, n):
        total = dnt[i] + down(i, rest)
        gtb[n] = total[0:D] * 64.0 - colt[:, i * STEP : (i + 1) * STEP].astype(F32) * total[D : D + 1]

    def turn(i, n):
        turned = gtb[n].T
        for s in range(2):
            cgf[2 * i + s] = turned[2 * s * OWN : (2 * s + 1) * OWN]
            cgx[2 * i + s] = turned[(2 * s + 1) * OWN : (2 * s + 2) * OWN].astype(BF16)

    def swap(i):
        pair = pl.ds(2 * i, 2)
        swaps[i] = send(cgx.at[pair], cgr.at[pair], core_peer)

    col_copies = []
    swaps = {}

    def add_cores(i):
        swaps[i].wait_recv()
        for k in (2 * i + 1, 2 * i):
            if k == 0:
                continue
            far, zrel = k // 8, ZREL[k % 8]
            cgs[k] = (cgf[k] + cgr[k].astype(F32)).astype(BF16)
            owner = at((h + far) % 2, (z + zrel + 8) % 8, c, x, l)
            col_copies.append((k, send(cgs.at[k], cgd.at[k], owner)))

    rest = slice(2 * STEP, ROWS)
    weigh(order[0], rest)
    for n, i in enumerate(order):
        if n < 7:
            weigh(order[n + 1], rest)
        across(i, rest)
        if n < EARLY:
            finish(i, n)
        if 0 < n <= EARLY:
            turn(order[n - 1], n - 1)
            swap(order[n - 1])
        if n > 3:
            add_cores(order[n - 4])

    sums = acr[:, D + 3 : D + 4]
    rgb[...] = (acr[:, 0:D] - rowe[...].astype(F32) * sums).astype(BF16)

    def placed(d):
        rows = slice(d * STEP, (d + 1) * STEP)
        return sum(
            jnp.dot(perm[i, rows, :], rgb[i * STEP : (i + 1) * STEP, :], preferred_element_type=F32) for i in range(4)
        )

    row_copies = {}
    for d in (2, 1, 3):
        rgs[d * STEP : (d + 1) * STEP, :] = placed(d).astype(BF16)
        row_copies[d] = scatter(d, rgs, rg_x)
    rgf[...] = placed(0)
    for n in range(4, EARLY):
        add_cores(order[n])
    for n in range(EARLY, 8):
        finish(order[n], n)
        turn(order[n], n)
        swap(order[n])
    for n in range(EARLY, 8):
        add_cores(order[n])

    row_last = reduce_rows(row_copies, rgf, rg_x, rg_s, rg_y)
    for copy in row_last:
        copy.wait_recv()
    row_total = rgf[0:OWN, :] + sum(rg_y[r].astype(F32) for r in range(3))
    out[0] = row_total * (2.0 / D)

    for k, copy in col_copies:
        copy.wait_recv()
    col_total = cgf[0] + cgr[0].astype(F32)
    for k, copy in col_copies:
        col_total += cgd[k].astype(F32)
    out[1] = col_total * (2.0 / D)
    for copy in sent:
        copy.wait_send()


def per_device(curve_embed, solution, targets, lengths, slot_curve, epoch_kernel):
    vmem = pl.BlockSpec(memory_space=pltpu.VMEM)
    scratch = [
        ((OWN, D), BF16), ((OWN, E), F32), ((OWN, E), BF16), ((1, OWN), I32), ((1, OWN), I32), ((E, E), F32),
        ((COLS, D + E), BF16), ((COLS, 2 * D), BF16), ((D, COLS), BF16), ((ROWS, D), BF16), ((ROWS, 2 * D), BF16),
        ((TURNED, ROWS), BF16), ((COLS // STEP, ROWS, STEP), F32), ((ROWS, E), F32), ((ROWS, E), BF16),
        ((12, OWN, E), BF16), ((3, OWN, E), BF16), ((3, OWN, E), BF16),
        ((ROWS, E), BF16), ((ROWS, 2 * D), F32), ((COLS // STEP, ROWS, STEP), BF16), ((16, 8, 128), I32), ((4, ROWS, STEP), BF16),
        ((COLS // STEP, TURNED, STEP), F32), ((8, D, STEP), F32),
        ((16, OWN, D), F32), ((16, OWN, D), BF16), ((16, OWN, D), BF16), ((16, OWN, D), BF16),
        ((16, OWN, D), BF16), ((ROWS, D), BF16), ((STEP, D), F32), ((ROWS, D), BF16),
        ((12, OWN, D), BF16), ((3, OWN, D), BF16), ((3, OWN, D), BF16),
    ]
    both = pl.pallas_call(
        kernel,
        out_shape=jax.ShapeDtypeStruct((2, OWN, D), F32),
        in_specs=[pl.BlockSpec(memory_space=pl.ANY)] * 6,
        out_specs=vmem,
        scratch_shapes=[pltpu.VMEM(s, t) for s, t in scratch]
        + [pltpu.SemaphoreType.DMA((160,)), pltpu.SemaphoreType.DMA((160,)), pltpu.SemaphoreType.DMA((6,))],
        compiler_params=pltpu.CompilerParams(
            collective_id=0, has_side_effects=True, vmem_limit_bytes=56 * 2**20
        ),
        name="tile",
    )(curve_embed, solution, targets, lengths.reshape(1, OWN), slot_curve.reshape(1, OWN), epoch_kernel)
    return both[0], both[1]


def solution(mesh):
    both = ("row", "col")
    return jax.shard_map(
        per_device,
        mesh=mesh,
        in_specs=(P(both, None), P(both, None), P(both, None), P(both), P(both), P()),
        out_specs=(P(both, None), P(both, None)),
        check_vma=False,
    )
```

```python
import jax
import jax.numpy as jnp
from jax import lax
from jax.experimental import pallas as pl
from jax.experimental.pallas import tpu as pltpu
from jax.sharding import PartitionSpec as P

MESH = pl.DeviceIdType.MESH
F32, BF16, I32 = jnp.float32, jnp.bfloat16, jnp.int32

OWN = 64
D = 128
E = 256
ROWS = 1024
COLS = 2048
ZREL = (0, 1, -1, 2, -2, 3, -3, 4)
ZSLOT = {z: k for k, z in enumerate(ZREL)}
ZSLOT[-4] = ZSLOT[4]
STEP = 256
EARLY = 6
PART = 512
TURNED = 144

NT = (((1,), (1,)), ((), ()))


def place():
    row, col = lax.axis_index("row"), lax.axis_index("col")
    return row // 16, (row // 2) % 8, row % 2, col // 4, col % 4


def at(h, z, c, x, l):
    return (h * 16 + z * 2 + c, x * 4 + l)


def pieces(wide):
    first = wide.astype(BF16).astype(F32)
    second = (wide - first).astype(BF16).astype(F32)
    third = (wide - first - second).astype(BF16).astype(F32)
    return first, second, third


def extended(embed, ones_first):
    wide = embed.astype(F32)
    squares = jnp.sum(wide * wide, axis=1, keepdims=True) * (-1.0 / D)
    a, b, c = pieces(squares)
    lane = lax.broadcasted_iota(I32, wide.shape, 1)
    at_parts = lane - 3 if ones_first else lane
    at_ones = lane if ones_first else lane - 3
    ones = jnp.where((at_ones >= 0) & (at_ones < 3), 1.0, 0.0)
    parts = jnp.where(at_parts == 0, a, jnp.where(at_parts == 1, b, jnp.where(at_parts == 2, c, ones)))
    return parts.astype(BF16)


def kernel(
    embed_hbm, solution_hbm, targets_hbm, lengths_hbm, ids_hbm, epoch_hbm,
    out,
    embed_ref, solution_ref, targets_ref, lengths_ref, ids_ref, epoch_ref,
    colb, cola, colt, rowe, rowa, rowt, kst, facc, fitb, fit_x, fit_s, fit_y,
    adjb, acr, wgt, idb, perm, dnt, gtb, cgf, cgx, cgr, cgs, cgd, rgb, rgf, rgs, rg_x, rg_s, rg_y,
    ssem, rsem, lsem,
):
    h, z, c, x, l = place()
    count = [0]
    sent = []

    def send(src, dst, device):
        i = count[0]
        count[0] += 1
        copy = pltpu.make_async_remote_copy(
            src_ref=src, dst_ref=dst, send_sem=ssem.at[i], recv_sem=rsem.at[i],
            device_id=device, device_id_type=MESH,
        )
        copy.start()
        sent.append(copy)
        return copy

    core_peer = at(h, z, 1 - c, x, l)
    far_peer = at(1 - h, z, c, x, 3 - l)
    z_peer = lambda d: at(h, (z + d + 8) % 8, c, x, l)
    plane_peer = lambda dx, dl: at(h, z, c, (x + dx + 4) % 4, (l + dl + 4) % 4)

    barrier = pltpu.get_barrier_semaphore()
    peers = [core_peer, far_peer] + [z_peer(d) for d in (1, -1, 2, -2)]
    peers += [plane_peer(d, 0) for d in (1, 2, 3)] + [plane_peer(0, d) for d in (1, 2, 3)]
    for peer in peers:
        pl.semaphore_signal(barrier, inc=1, device_id=peer, device_id_type=MESH)

    loads = [
        pltpu.make_async_copy(src, dst, lsem.at[i])
        for i, (src, dst) in enumerate([
            (solution_hbm, solution_ref), (epoch_hbm, epoch_ref), (embed_hbm, embed_ref),
            (ids_hbm, ids_ref), (targets_hbm, targets_ref), (lengths_hbm, lengths_ref),
        ])
    ]
    for load in loads:
        load.start()
    for load in loads[:4]:
        load.wait()

    def block(slot):
        return pl.ds(slot * OWN, OWN)

    fitted = jnp.dot(
        solution_ref[...], epoch_ref[...], precision=lax.Precision.HIGHEST, preferred_element_type=F32
    )
    colb[0:OWN, 0:D] = embed_ref[...]
    colb[0:OWN, D : D + E] = fitted.astype(BF16)
    rowe[0:OWN, :] = embed_ref[...]
    ids = ids_ref[...]
    idb[0] = jnp.broadcast_to(jnp.concatenate([ids, ids], axis=1), (8, 128))
    pl.semaphore_wait(barrier, len(peers))

    def slot_of(far, zrel, other):
        return far * 16 + ZSLOT[zrel] * 2 + other

    came = {}

    def forward(far, zrel, steps):
        for step in steps:
            goal = zrel - step
            came[far, ZSLOT[goal]] = send(
                colb.at[block(slot_of(far, zrel, 0)), :], colb.at[block(slot_of(far, goal, 0)), :], z_peer(step)
            )

    def share(far, zrel):
        came[far, ZSLOT[zrel], "core"] = send(
            colb.at[block(slot_of(far, zrel, 0)), :], colb.at[block(slot_of(far, zrel, 1)), :], core_peer
        )

    def arrive(far, zrel):
        came[far, ZSLOT[zrel]].wait_recv()
        share(far, zrel)

    far_copy = send(colb.at[block(0), :], colb.at[block(16), :], far_peer)
    forward(0, 0, (1, -1, 2, -2))
    share(0, 0)

    def gather_rows(ref):
        along_l = [send(ref(0), ref(d), plane_peer(0, -d)) for d in (1, 2, 3)]
        along_x = {}

        def go(e, d):
            along_x[e, d] = send(ref(d), ref(e * 4 + d), plane_peer(-e, 0))

        for e in (1, 3, 2):
            go(e, 0)

        def spread():
            for d, copy in zip((1, 2, 3), along_l):
                copy.wait_recv()
                go(1, d), go(3, d)
            for d in (1, 2, 3):
                go(2, d)

        def finish(e):
            for d in range(4):
                along_x[e, d].wait_recv()

        return spread, finish

    spread_rows, finish_rows = gather_rows(lambda s: rowe.at[block(s), :])

    arrive(0, -1), arrive(0, 1)
    spread_rows()
    arrive(0, -2)
    forward(0, -2, (2, 1))
    arrive(0, 2)
    forward(0, 2, (-1,))
    far_copy.wait_recv()
    forward(1, 0, (-2, 2, -1, 1))
    share(1, 0)
    for e in (1, 2, 3):
        finish_rows(e)
    id_copies = [send(idb.at[0], idb.at[s], plane_peer(-(s // 4), -(s % 4))) for s in range(1, 16)]
    rowe_all = rowe[...]
    rowa[:, 0:D] = (rowe_all.astype(F32) * (1.0 / 64)).astype(BF16)
    rowa[:, D:] = extended(rowe_all, True)

    def columns_in(part):
        for k in range(4 * part, 4 * part + 4):
            came[k // 8, k % 8, "core"].wait_recv()
        cols = slice(part * PART, (part + 1) * PART)
        embed = colb[cols, 0:D]
        cola[cols, 0:D] = embed
        cola[cols, D:] = extended(embed, False)

    def kernel_rows(part, r):
        rows = slice(r * STEP, (r + 1) * STEP)
        cols = slice(part * PART, (part + 1) * PART)
        kern = jnp.exp(lax.dot_general(rowa[rows, :], cola[cols, :], NT, preferred_element_type=F32))
        kst[2 * part, rows, :] = kern[:, 0:STEP]
        kst[2 * part + 1, rows, :] = kern[:, STEP:PART]

    def fit_rows(part, r):
        rows = slice(r * STEP, (r + 1) * STEP)
        total = None if part == 0 else facc[rows, :]
        for i in (2 * part, 2 * part + 1):
            field = colb[i * STEP : (i + 1) * STEP, D : D + E]
            one = jnp.dot(kst[i, rows, :].astype(BF16), field, preferred_element_type=F32)
            total = one if total is None else total + one
        facc[rows, :] = total

    def fit_part(part, done=lambda r: None):
        columns_in(part)
        order = (2, 1, 3, 0)
        kernel_rows(part, order[0])
        for n, r in enumerate(order):
            if n < 3:
                kernel_rows(part, order[n + 1])
            fit_rows(part, r)
            done(r)

    fit_part(0)
    arrive(1, 2)
    forward(1, 2, (-2, -1))
    arrive(1, -2)
    forward(1, -2, (1,))
    arrive(1, -1), arrive(1, 1)
    arrive(0, -3), arrive(0, 3), arrive(0, 4)
    fit_part(2)
    fit_part(1)
    arrive(1, -3), arrive(1, 3), arrive(1, 4)

    def scatter(d, ref, got):
        return {r: send(ref.at[block(4 * d + r), :], got.at[4 * (d - 1) + r], plane_peer(d, 0)) for r in (2, 1, 3, 0)}

    def reduce_rows(copies, mine, got, going, ends):
        last = []
        for r in (2, 1, 3, 0):
            for d in (2, 1, 3):
                copies[d][r].wait_recv()
            rows = block(r)
            mine[rows, :] += sum(got[4 * d + r].astype(F32) for d in range(3))
            if r:
                going[r - 1] = mine[rows, :].astype(BF16)
                last.append(send(going.at[r - 1], ends.at[r - 1], plane_peer(0, r)))
        return last

    passing, below, above = {}, {}, {}

    def put(d, r, slot, step):
        return send(fitb.at[block(4 * d + r), :], fit_x.at[slot], plane_peer(step, 0))

    def leave(d):
        if d == 2:
            rows = slice(d * STEP, (d + 1) * STEP)
            fitb[rows, :] = facc[rows, :].astype(BF16)
            for r in (2, 3, 1, 0):
                passing[r] = put(2, r, 8 + r, 1 if r in (1, 2) else -1)
        if d == 1:
            for r in (3, 0):
                fitb[block(4 + r), :] = facc[block(4 + r), :].astype(BF16)
                below[r] = put(1, r, r, 1)
        if d == 3:
            for r in (2, 1):
                fitb[block(12 + r), :] = facc[block(12 + r), :].astype(BF16)
                above[r] = put(3, r, 4 + r, -1)

    fit_part(3, leave)
    for r in (2, 3, 1, 0):
        passing[r].wait_recv()
        d = 1 if r in (1, 2) else 3
        fitb[block(4 * d + r), :] = (facc[block(4 * d + r), :] + fit_x[8 + r].astype(F32)).astype(BF16)
        if d == 1:
            below[r] = put(1, r, r, 1)
        else:
            above[r] = put(3, r, 4 + r, -1)
    fit_last = []
    for r in (2, 3, 1, 0):
        below[r].wait_recv()
        above[r].wait_recv()
        facc[block(r), :] += fit_x[r].astype(F32) + fit_x[4 + r].astype(F32)
        if r:
            fit_s[r - 1] = facc[block(r), :].astype(BF16)
            fit_last.append(send(fit_s.at[r - 1], fit_y.at[r - 1], plane_peer(0, r)))

    rowt[...] = rowa[...].T[0:TURNED]
    colt[...] = colb[:, 0:D].T
    for copy in id_copies:
        copy.wait_recv()
    lane = lax.broadcasted_iota(I32, (1, 128), 1)

    @pl.loop(0, 8)
    def _(i):
        both = jnp.where(lane < OWN, idb[2 * i, 0:1, :], idb[2 * i + 1, 0:1, :])
        across_x = (((both >> 8) & 3) - x) & 3
        across_l = (((both >> 6) & 3) - l) & 3
        goal = across_x * 256 + across_l * OWN + (both & (OWN - 1))
        seat = lax.broadcasted_iota(I32, (ROWS, 128), 0)
        perm[i // 2, :, pl.ds(pl.multiple_of((i % 2) * 128, 128), 128)] = jnp.where(seat == goal, 1.0, 0.0).astype(BF16)

    for load in loads[4:]:
        load.wait()
    diagonal = lax.broadcasted_iota(I32, (OWN, OWN), 0) == lax.broadcasted_iota(I32, (OWN, OWN), 1)
    spans = jnp.broadcast_to(lengths_ref[...].astype(F32), (OWN, OWN))
    span = jnp.sum(jnp.where(diagonal, spans, 0.0), axis=1, keepdims=True)
    epoch = lax.broadcasted_iota(I32, (OWN, E), 1).astype(F32)

    total = facc[0:OWN, :]
    for copy in fit_last:
        copy.wait_recv()
    total += sum(fit_y[r].astype(F32) for r in range(3))
    adjoint = jnp.where(epoch < span, targets_ref[...].astype(F32) - total, 0.0).astype(BF16)
    adjb[0:OWN, :] = adjoint
    spread_adjoint, finish_adjoint = gather_rows(lambda s: adjb.at[block(s), :])
    spread_adjoint()

    def weigh(i, rows):
        cols = slice(i * STEP, (i + 1) * STEP)
        link = lax.dot_general(adjb[rows, :], colb[cols, D : D + E], NT, preferred_element_type=F32)
        wgt[i, rows, :] = (link * kst[i, rows, :]).astype(BF16)

    def across(i, rows):
        part = jnp.dot(wgt[i, rows, :], cola[i * STEP : (i + 1) * STEP, :], preferred_element_type=F32)
        if i == order[0]:
            acr[rows, :] = part
        else:
            acr[rows, :] += part

    def down(i, rows):
        return jnp.dot(rowt[:, rows], wgt[i, rows, :], preferred_element_type=F32)

    order = (7, 6, 5, 4, 3, 2, 1, 0)

    def rows_arrived(e):
        rows = slice(e * STEP, (e + 1) * STEP)
        weigh(order[0], rows)
        for n, i in enumerate(order):
            if n < 7:
                weigh(order[n + 1], rows)
            across(i, rows)
            part = down(i, rows)
            if e == 0:
                dnt[i] = part
            else:
                dnt[i] += part

    rows_arrived(0)
    finish_adjoint(1)
    rows_arrived(1)
    finish_adjoint(3)
    finish_adjoint(2)

    def finish(i, n):
        total = dnt[i] + down(i, rest)
        gtb[n] = total[0:D] * 64.0 - colt[:, i * STEP : (i + 1) * STEP].astype(F32) * total[D : D + 1]

    def turn(i, n):
        turned = gtb[n].T
        for s in range(2):
            cgf[2 * i + s] = turned[2 * s * OWN : (2 * s + 1) * OWN]
            cgx[2 * i + s] = turned[(2 * s + 1) * OWN : (2 * s + 2) * OWN].astype(BF16)

    def swap(i):
        pair = pl.ds(2 * i, 2)
        swaps[i] = send(cgx.at[pair], cgr.at[pair], core_peer)

    col_copies = []
    swaps = {}

    def add_cores(i):
        swaps[i].wait_recv()
        for k in (2 * i + 1, 2 * i):
            if k == 0:
                continue
            far, zrel = k // 8, ZREL[k % 8]
            cgs[k] = (cgf[k] + cgr[k].astype(F32)).astype(BF16)
            owner = at((h + far) % 2, (z + zrel + 8) % 8, c, x, 3 - l if far else l)
            col_copies.append((k, send(cgs.at[k], cgd.at[k], owner)))

    rest = slice(2 * STEP, ROWS)
    weigh(order[0], rest)
    for n, i in enumerate(order):
        if n < 7:
            weigh(order[n + 1], rest)
        across(i, rest)
        if n < EARLY:
            finish(i, n)
        if 0 < n <= EARLY:
            turn(order[n - 1], n - 1)
            swap(order[n - 1])

    for i in order[:4]:
        add_cores(i)
    sums = acr[:, D + 3 : D + 4]
    rgb[...] = (acr[:, 0:D] - rowe[...].astype(F32) * sums).astype(BF16)

    def placed(d):
        rows = slice(d * STEP, (d + 1) * STEP)
        return sum(
            jnp.dot(perm[i, rows, :], rgb[i * STEP : (i + 1) * STEP, :], preferred_element_type=F32) for i in range(4)
        )

    row_copies = {}
    for d in (2, 1, 3):
        rgs[d * STEP : (d + 1) * STEP, :] = placed(d).astype(BF16)
        row_copies[d] = scatter(d, rgs, rg_x)
    rgf[...] = placed(0)
    for n in range(4, EARLY):
        add_cores(order[n])
    for n in range(EARLY, 8):
        finish(order[n], n)
        turn(order[n], n)
        swap(order[n])
    for n in range(EARLY, 8):
        add_cores(order[n])

    row_last = reduce_rows(row_copies, rgf, rg_x, rg_s, rg_y)
    for copy in row_last:
        copy.wait_recv()
    row_total = rgf[0:OWN, :] + sum(rg_y[r].astype(F32) for r in range(3))
    out[0] = row_total * (2.0 / D)

    for k, copy in col_copies:
        copy.wait_recv()
    col_total = cgf[0] + cgr[0].astype(F32)
    for k, copy in col_copies:
        col_total += cgd[k].astype(F32)
    out[1] = col_total * (2.0 / D)
    for copy in sent:
        copy.wait_send()


def per_device(curve_embed, solution, targets, lengths, slot_curve, epoch_kernel):
    vmem = pl.BlockSpec(memory_space=pltpu.VMEM)
    scratch = [
        ((OWN, D), BF16), ((OWN, E), F32), ((OWN, E), BF16), ((1, OWN), I32), ((1, OWN), I32), ((E, E), F32),
        ((COLS, D + E), BF16), ((COLS, 2 * D), BF16), ((D, COLS), BF16), ((ROWS, D), BF16), ((ROWS, 2 * D), BF16),
        ((TURNED, ROWS), BF16), ((COLS // STEP, ROWS, STEP), F32), ((ROWS, E), F32), ((ROWS, E), BF16),
        ((12, OWN, E), BF16), ((3, OWN, E), BF16), ((3, OWN, E), BF16),
        ((ROWS, E), BF16), ((ROWS, 2 * D), F32), ((COLS // STEP, ROWS, STEP), BF16), ((16, 8, 128), I32), ((4, ROWS, STEP), BF16),
        ((COLS // STEP, TURNED, STEP), F32), ((8, D, STEP), F32),
        ((16, OWN, D), F32), ((16, OWN, D), BF16), ((16, OWN, D), BF16), ((16, OWN, D), BF16),
        ((16, OWN, D), BF16), ((ROWS, D), BF16), ((STEP, D), F32), ((ROWS, D), BF16),
        ((12, OWN, D), BF16), ((3, OWN, D), BF16), ((3, OWN, D), BF16),
    ]
    both = pl.pallas_call(
        kernel,
        out_shape=jax.ShapeDtypeStruct((2, OWN, D), F32),
        in_specs=[pl.BlockSpec(memory_space=pl.ANY)] * 6,
        out_specs=vmem,
        scratch_shapes=[pltpu.VMEM(s, t) for s, t in scratch]
        + [pltpu.SemaphoreType.DMA((160,)), pltpu.SemaphoreType.DMA((160,)), pltpu.SemaphoreType.DMA((6,))],
        compiler_params=pltpu.CompilerParams(
            collective_id=0, has_side_effects=True, vmem_limit_bytes=56 * 2**20
        ),
        name="tile",
    )(curve_embed, solution, targets, lengths.reshape(1, OWN), slot_curve.reshape(1, OWN), epoch_kernel)
    return both[0], both[1]


def solution(mesh):
    both = ("row", "col")
    return jax.shard_map(
        per_device,
        mesh=mesh,
        in_specs=(P(both, None), P(both, None), P(both, None), P(both), P(both), P()),
        out_specs=(P(both, None), P(both, None)),
        check_vma=False,
    )
```

```python
import jax
import jax.numpy as jnp
from jax import lax
from jax.experimental import pallas as pl
from jax.experimental.pallas import tpu as pltpu
from jax.sharding import PartitionSpec as P

MESH = pl.DeviceIdType.MESH
F32, BF16, I32 = jnp.float32, jnp.bfloat16, jnp.int32

OWN = 64
D = 128
E = 256
ROWS = 1024
COLS = 2048
ZREL = (0, 1, -1, 2, -2, 3, -3, 4)
ZSLOT = {z: k for k, z in enumerate(ZREL)}
ZSLOT[-4] = ZSLOT[4]
STEP = 256
EARLY = 6
PART = 512
TURNED = 144

NT = (((1,), (1,)), ((), ()))


def place():
    row, col = lax.axis_index("row"), lax.axis_index("col")
    return row // 16, (row // 2) % 8, row % 2, col // 4, col % 4


def at(h, z, c, x, l):
    return (h * 16 + z * 2 + c, x * 4 + l)


def pieces(wide):
    first = wide.astype(BF16).astype(F32)
    second = (wide - first).astype(BF16).astype(F32)
    third = (wide - first - second).astype(BF16).astype(F32)
    return first, second, third


def extended(embed, ones_first):
    wide = embed.astype(F32)
    squares = jnp.sum(wide * wide, axis=1, keepdims=True) * (-1.0 / D)
    a, b, c = pieces(squares)
    lane = lax.broadcasted_iota(I32, wide.shape, 1)
    at_parts = lane - 3 if ones_first else lane
    at_ones = lane if ones_first else lane - 3
    ones = jnp.where((at_ones >= 0) & (at_ones < 3), 1.0, 0.0)
    parts = jnp.where(at_parts == 0, a, jnp.where(at_parts == 1, b, jnp.where(at_parts == 2, c, ones)))
    return parts.astype(BF16)


def kernel(
    embed_hbm, solution_hbm, targets_hbm, lengths_hbm, ids_hbm, epoch_hbm,
    out,
    embed_ref, solution_ref, targets_ref, lengths_ref, ids_ref, epoch_ref,
    colb, cola, colt, rowe, rowa, rowt, kst, facc, fitb, fit_x, fit_s, fit_y,
    adjb, acr, wgt, idb, perm, dnt, gtb, cgf, cgx, cgr, cgs, cgd, rgb, rgf, rgs, rg_x, rg_s, rg_y,
    ssem, rsem, lsem,
):
    h, z, c, x, l = place()
    count = [0]
    sent = []

    def send(src, dst, device):
        i = count[0]
        count[0] += 1
        copy = pltpu.make_async_remote_copy(
            src_ref=src, dst_ref=dst, send_sem=ssem.at[i], recv_sem=rsem.at[i],
            device_id=device, device_id_type=MESH,
        )
        copy.start()
        sent.append(copy)
        return copy

    core_peer = at(h, z, 1 - c, x, l)
    far_peer = at(1 - h, z, c, x, 3 - l)
    z_peer = lambda d: at(h, (z + d + 8) % 8, c, x, l)
    plane_peer = lambda dx, dl: at(h, z, c, (x + dx + 4) % 4, (l + dl + 4) % 4)

    barrier = pltpu.get_barrier_semaphore()
    peers = [core_peer, far_peer] + [z_peer(d) for d in (1, -1, 2, -2)]
    peers += [plane_peer(d, 0) for d in (1, 2, 3)] + [plane_peer(0, d) for d in (1, 2, 3)]
    for peer in peers:
        pl.semaphore_signal(barrier, inc=1, device_id=peer, device_id_type=MESH)

    loads = [
        pltpu.make_async_copy(src, dst, lsem.at[i])
        for i, (src, dst) in enumerate([
            (solution_hbm, solution_ref), (epoch_hbm, epoch_ref), (embed_hbm, embed_ref),
            (ids_hbm, ids_ref), (targets_hbm, targets_ref), (lengths_hbm, lengths_ref),
        ])
    ]
    for load in loads:
        load.start()
    for load in loads[:4]:
        load.wait()

    def block(slot):
        return pl.ds(slot * OWN, OWN)

    fitted = jnp.dot(
        solution_ref[...], epoch_ref[...], precision=lax.Precision.HIGHEST, preferred_element_type=F32
    )
    colb[0:OWN, 0:D] = embed_ref[...]
    colb[0:OWN, D : D + E] = fitted.astype(BF16)
    rowe[0:OWN, :] = embed_ref[...]
    ids = ids_ref[...]
    idb[0] = jnp.broadcast_to(jnp.concatenate([ids, ids], axis=1), (8, 128))
    pl.semaphore_wait(barrier, len(peers))

    def slot_of(far, zrel, other):
        return far * 16 + ZSLOT[zrel] * 2 + other

    came = {}

    def forward(far, zrel, steps):
        for step in steps:
            goal = zrel - step
            came[far, ZSLOT[goal]] = send(
                colb.at[block(slot_of(far, zrel, 0)), :], colb.at[block(slot_of(far, goal, 0)), :], z_peer(step)
            )

    def share(far, zrel):
        came[far, ZSLOT[zrel], "core"] = send(
            colb.at[block(slot_of(far, zrel, 0)), :], colb.at[block(slot_of(far, zrel, 1)), :], core_peer
        )

    def arrive(far, zrel):
        came[far, ZSLOT[zrel]].wait_recv()
        share(far, zrel)

    far_copy = send(colb.at[block(0), :], colb.at[block(16), :], far_peer)
    forward(0, 0, (1, -1, 2, -2))
    share(0, 0)

    def gather_rows(ref):
        along_l = [send(ref(0), ref(d), plane_peer(0, -d)) for d in (1, 2, 3)]
        along_x = {}

        def go(e, d):
            along_x[e, d] = send(ref(d), ref(e * 4 + d), plane_peer(-e, 0))

        for e in (1, 3, 2):
            go(e, 0)

        def spread():
            for d, copy in zip((1, 2, 3), along_l):
                copy.wait_recv()
                go(1, d), go(3, d)
            for d in (1, 2, 3):
                go(2, d)

        def finish(e):
            for d in range(4):
                along_x[e, d].wait_recv()

        return spread, finish

    spread_rows, finish_rows = gather_rows(lambda s: rowe.at[block(s), :])

    arrive(0, -1), arrive(0, 1)
    spread_rows()
    arrive(0, -2)
    forward(0, -2, (2, 1))
    arrive(0, 2)
    forward(0, 2, (-1,))
    far_copy.wait_recv()
    forward(1, 0, (-2, 2, -1, 1))
    share(1, 0)
    for e in (1, 2, 3):
        finish_rows(e)
    id_copies = [send(idb.at[0], idb.at[s], plane_peer(-(s // 4), -(s % 4))) for s in range(1, 16)]
    rowe_all = rowe[...]
    rowa[:, 0:D] = (rowe_all.astype(F32) * (1.0 / 64)).astype(BF16)
    rowa[:, D:] = extended(rowe_all, True)

    def columns_in(part):
        for k in range(4 * part, 4 * part + 4):
            came[k // 8, k % 8, "core"].wait_recv()
        cols = slice(part * PART, (part + 1) * PART)
        embed = colb[cols, 0:D]
        cola[cols, 0:D] = embed
        cola[cols, D:] = extended(embed, False)

    def kernel_rows(part, r):
        rows = slice(r * STEP, (r + 1) * STEP)
        cols = slice(part * PART, (part + 1) * PART)
        kern = jnp.exp(lax.dot_general(rowa[rows, :], cola[cols, :], NT, preferred_element_type=F32))
        kst[2 * part, rows, :] = kern[:, 0:STEP]
        kst[2 * part + 1, rows, :] = kern[:, STEP:PART]

    def fit_rows(part, r):
        rows = slice(r * STEP, (r + 1) * STEP)
        total = None if part == 0 else facc[rows, :]
        for i in (2 * part, 2 * part + 1):
            field = colb[i * STEP : (i + 1) * STEP, D : D + E]
            one = jnp.dot(kst[i, rows, :].astype(BF16), field, preferred_element_type=F32)
            total = one if total is None else total + one
        facc[rows, :] = total

    def fit_part(part, done=lambda r: None):
        columns_in(part)
        order = (2, 1, 3, 0)
        kernel_rows(part, order[0])
        for n, r in enumerate(order):
            if n < 3:
                kernel_rows(part, order[n + 1])
            fit_rows(part, r)
            done(r)

    fit_part(0)
    arrive(1, 2)
    forward(1, 2, (-2, -1))
    arrive(1, -2)
    forward(1, -2, (1,))
    arrive(1, -1), arrive(1, 1)
    arrive(0, -3), arrive(0, 3), arrive(0, 4)
    fit_part(2)
    fit_part(1)
    arrive(1, -3), arrive(1, 3), arrive(1, 4)

    def scatter(d, ref, got):
        return {r: send(ref.at[block(4 * d + r), :], got.at[4 * (d - 1) + r], plane_peer(d, 0)) for r in (2, 1, 3, 0)}

    def reduce_rows(copies, mine, got, going, ends):
        last = []
        for r in (2, 1, 3, 0):
            for d in (2, 1, 3):
                copies[d][r].wait_recv()
            rows = block(r)
            mine[rows, :] += sum(got[4 * d + r].astype(F32) for d in range(3))
            if r:
                going[r - 1] = mine[rows, :].astype(BF16)
                last.append(send(going.at[r - 1], ends.at[r - 1], plane_peer(0, r)))
        return last

    passing, below, above = {}, {}, {}

    def put(d, r, slot, step):
        return send(fitb.at[block(4 * d + r), :], fit_x.at[slot], plane_peer(step, 0))

    def leave(d):
        if d == 2:
            rows = slice(d * STEP, (d + 1) * STEP)
            fitb[rows, :] = facc[rows, :].astype(BF16)
            for r in (2, 3, 1, 0):
                passing[r] = put(2, r, 8 + r, 1 if r in (1, 2) else -1)
        if d == 1:
            for r in (3, 0):
                fitb[block(4 + r), :] = facc[block(4 + r), :].astype(BF16)
                below[r] = put(1, r, r, 1)
        if d == 3:
            for r in (2, 1):
                fitb[block(12 + r), :] = facc[block(12 + r), :].astype(BF16)
                above[r] = put(3, r, 4 + r, -1)

    fit_part(3, leave)
    for r in (2, 3, 1, 0):
        passing[r].wait_recv()
        d = 1 if r in (1, 2) else 3
        fitb[block(4 * d + r), :] = (facc[block(4 * d + r), :] + fit_x[8 + r].astype(F32)).astype(BF16)
        if d == 1:
            below[r] = put(1, r, r, 1)
        else:
            above[r] = put(3, r, 4 + r, -1)
    fit_last = []
    for r in (2, 3, 1, 0):
        below[r].wait_recv()
        above[r].wait_recv()
        facc[block(r), :] += fit_x[r].astype(F32) + fit_x[4 + r].astype(F32)
        if r:
            fit_s[r - 1] = facc[block(r), :].astype(BF16)
            fit_last.append(send(fit_s.at[r - 1], fit_y.at[r - 1], plane_peer(0, r)))

    rowt[...] = rowa[...].T[0:TURNED]
    colt[...] = colb[:, 0:D].T
    for copy in id_copies:
        copy.wait_recv()
    lane = lax.broadcasted_iota(I32, (1, 128), 1)

    @pl.loop(0, 8)
    def _(i):
        both = jnp.where(lane < OWN, idb[2 * i, 0:1, :], idb[2 * i + 1, 0:1, :])
        across_x = (((both >> 8) & 3) - x) & 3
        across_l = (((both >> 6) & 3) - l) & 3
        goal = across_x * 256 + across_l * OWN + (both & (OWN - 1))
        seat = lax.broadcasted_iota(I32, (ROWS, 128), 0)
        perm[i // 2, :, pl.ds(pl.multiple_of((i % 2) * 128, 128), 128)] = jnp.where(seat == goal, 1.0, 0.0).astype(BF16)

    for load in loads[4:]:
        load.wait()
    diagonal = lax.broadcasted_iota(I32, (OWN, OWN), 0) == lax.broadcasted_iota(I32, (OWN, OWN), 1)
    spans = jnp.broadcast_to(lengths_ref[...].astype(F32), (OWN, OWN))
    span = jnp.sum(jnp.where(diagonal, spans, 0.0), axis=1, keepdims=True)
    epoch = lax.broadcasted_iota(I32, (OWN, E), 1).astype(F32)

    total = facc[0:OWN, :]
    for copy in fit_last:
        copy.wait_recv()
    total += sum(fit_y[r].astype(F32) for r in range(3))
    adjoint = jnp.where(epoch < span, targets_ref[...].astype(F32) - total, 0.0).astype(BF16)
    adjb[0:OWN, :] = adjoint
    spread_adjoint, finish_adjoint = gather_rows(lambda s: adjb.at[block(s), :])
    spread_adjoint()

    def weigh(i, rows):
        cols = slice(i * STEP, (i + 1) * STEP)
        link = lax.dot_general(adjb[rows, :], colb[cols, D : D + E], NT, preferred_element_type=F32)
        wgt[i, rows, :] = (link * kst[i, rows, :]).astype(BF16)

    def across(i, rows):
        part = jnp.dot(wgt[i, rows, :], cola[i * STEP : (i + 1) * STEP, :], preferred_element_type=F32)
        if i == order[0]:
            acr[rows, :] = part
        else:
            acr[rows, :] += part

    def down(i, rows):
        return jnp.dot(rowt[:, rows], wgt[i, rows, :], preferred_element_type=F32)

    order = (7, 6, 5, 4, 3, 2, 1, 0)

    def rows_arrived(e):
        rows = slice(e * STEP, (e + 1) * STEP)
        weigh(order[0], rows)
        for n, i in enumerate(order):
            if n < 7:
                weigh(order[n + 1], rows)
            across(i, rows)
            part = down(i, rows)
            if e == 0:
                dnt[i] = part
            else:
                dnt[i] += part

    rows_arrived(0)
    finish_adjoint(1)
    rows_arrived(1)
    finish_adjoint(3)
    finish_adjoint(2)

    def finish(i, n):
        total = dnt[i] + down(i, rest)
        gtb[n] = total[0:D] * 64.0 - colt[:, i * STEP : (i + 1) * STEP].astype(F32) * total[D : D + 1]

    def turn(i, n):
        turned = gtb[n].T
        for s in range(2):
            cgf[2 * i + s] = turned[2 * s * OWN : (2 * s + 1) * OWN]
            cgx[2 * i + s] = turned[(2 * s + 1) * OWN : (2 * s + 2) * OWN].astype(BF16)

    def swap(i):
        pair = pl.ds(2 * i, 2)
        swaps[i] = send(cgx.at[pair], cgr.at[pair], core_peer)

    col_copies = []
    swaps = {}

    def add_cores(i):
        swaps[i].wait_recv()
        for k in (2 * i + 1, 2 * i):
            if k == 0:
                continue
            far, zrel = k // 8, ZREL[k % 8]
            cgs[k] = (cgf[k] + cgr[k].astype(F32)).astype(BF16)
            owner = at((h + far) % 2, (z + zrel + 8) % 8, c, x, 3 - l if far else l)
            col_copies.append((k, send(cgs.at[k], cgd.at[k], owner)))

    rest = slice(2 * STEP, ROWS)
    weigh(order[0], rest)
    for n, i in enumerate(order):
        if n < 7:
            weigh(order[n + 1], rest)
        across(i, rest)
        if n < EARLY:
            finish(i, n)
        if 0 < n <= EARLY:
            turn(order[n - 1], n - 1)
            swap(order[n - 1])

    sums = acr[:, D + 3 : D + 4]
    rgb[...] = (acr[:, 0:D] - rowe[...].astype(F32) * sums).astype(BF16)

    def placed(d):
        rows = slice(d * STEP, (d + 1) * STEP)
        return sum(
            jnp.dot(perm[i, rows, :], rgb[i * STEP : (i + 1) * STEP, :], preferred_element_type=F32) for i in range(4)
        )

    row_copies = {}
    for d in (2, 1, 3):
        rgs[d * STEP : (d + 1) * STEP, :] = placed(d).astype(BF16)
        row_copies[d] = scatter(d, rgs, rg_x)
    rgf[...] = placed(0)
    for n in range(EARLY):
        add_cores(order[n])
    for n in range(EARLY, 8):
        finish(order[n], n)
        turn(order[n], n)
        swap(order[n])
    for n in range(EARLY, 8):
        add_cores(order[n])

    row_last = reduce_rows(row_copies, rgf, rg_x, rg_s, rg_y)
    for copy in row_last:
        copy.wait_recv()
    row_total = rgf[0:OWN, :] + sum(rg_y[r].astype(F32) for r in range(3))
    out[0] = row_total * (2.0 / D)

    for k, copy in col_copies:
        copy.wait_recv()
    col_total = cgf[0] + cgr[0].astype(F32)
    for k, copy in col_copies:
        col_total += cgd[k].astype(F32)
    out[1] = col_total * (2.0 / D)
    for copy in sent:
        copy.wait_send()


def per_device(curve_embed, solution, targets, lengths, slot_curve, epoch_kernel):
    vmem = pl.BlockSpec(memory_space=pltpu.VMEM)
    scratch = [
        ((OWN, D), BF16), ((OWN, E), F32), ((OWN, E), BF16), ((1, OWN), I32), ((1, OWN), I32), ((E, E), F32),
        ((COLS, D + E), BF16), ((COLS, 2 * D), BF16), ((D, COLS), BF16), ((ROWS, D), BF16), ((ROWS, 2 * D), BF16),
        ((TURNED, ROWS), BF16), ((COLS // STEP, ROWS, STEP), F32), ((ROWS, E), F32), ((ROWS, E), BF16),
        ((12, OWN, E), BF16), ((3, OWN, E), BF16), ((3, OWN, E), BF16),
        ((ROWS, E), BF16), ((ROWS, 2 * D), F32), ((COLS // STEP, ROWS, STEP), BF16), ((16, 8, 128), I32), ((4, ROWS, STEP), BF16),
        ((COLS // STEP, TURNED, STEP), F32), ((8, D, STEP), F32),
        ((16, OWN, D), F32), ((16, OWN, D), BF16), ((16, OWN, D), BF16), ((16, OWN, D), BF16),
        ((16, OWN, D), BF16), ((ROWS, D), BF16), ((STEP, D), F32), ((ROWS, D), BF16),
        ((12, OWN, D), BF16), ((3, OWN, D), BF16), ((3, OWN, D), BF16),
    ]
    both = pl.pallas_call(
        kernel,
        out_shape=jax.ShapeDtypeStruct((2, OWN, D), F32),
        in_specs=[pl.BlockSpec(memory_space=pl.ANY)] * 6,
        out_specs=vmem,
        scratch_shapes=[pltpu.VMEM(s, t) for s, t in scratch]
        + [pltpu.SemaphoreType.DMA((160,)), pltpu.SemaphoreType.DMA((160,)), pltpu.SemaphoreType.DMA((6,))],
        compiler_params=pltpu.CompilerParams(
            collective_id=0, has_side_effects=True, vmem_limit_bytes=56 * 2**20
        ),
        name="tile",
    )(curve_embed, solution, targets, lengths.reshape(1, OWN), slot_curve.reshape(1, OWN), epoch_kernel)
    return both[0], both[1]


def solution(mesh):
    both = ("row", "col")
    return jax.shard_map(
        per_device,
        mesh=mesh,
        in_specs=(P(both, None), P(both, None), P(both, None), P(both), P(both), P()),
        out_specs=(P(both, None), P(both, None)),
        check_vma=False,
    )
```

```python
import jax
import jax.numpy as jnp
from jax import lax
from jax.experimental import pallas as pl
from jax.experimental.pallas import tpu as pltpu
from jax.sharding import PartitionSpec as P

MESH = pl.DeviceIdType.MESH
F32, BF16, I32 = jnp.float32, jnp.bfloat16, jnp.int32

OWN = 64
D = 128
E = 256
ROWS = 1024
COLS = 2048
ZREL = (0, 1, -1, 2, -2, 3, -3, 4)
ZSLOT = {z: k for k, z in enumerate(ZREL)}
ZSLOT[-4] = ZSLOT[4]
STEP = 256
EARLY = 4
PART = 512
TURNED = 144

NT = (((1,), (1,)), ((), ()))


def place():
    row, col = lax.axis_index("row"), lax.axis_index("col")
    return row // 16, (row // 2) % 8, row % 2, col // 4, col % 4


def at(h, z, c, x, l):
    return (h * 16 + z * 2 + c, x * 4 + l)


def pieces(wide):
    first = wide.astype(BF16).astype(F32)
    second = (wide - first).astype(BF16).astype(F32)
    third = (wide - first - second).astype(BF16).astype(F32)
    return first, second, third


def extended(embed, ones_first):
    wide = embed.astype(F32)
    squares = jnp.sum(wide * wide, axis=1, keepdims=True) * (-1.0 / D)
    a, b, c = pieces(squares)
    lane = lax.broadcasted_iota(I32, wide.shape, 1)
    at_parts = lane - 3 if ones_first else lane
    at_ones = lane if ones_first else lane - 3
    ones = jnp.where((at_ones >= 0) & (at_ones < 3), 1.0, 0.0)
    parts = jnp.where(at_parts == 0, a, jnp.where(at_parts == 1, b, jnp.where(at_parts == 2, c, ones)))
    return parts.astype(BF16)


def kernel(
    embed_hbm, solution_hbm, targets_hbm, lengths_hbm, ids_hbm, epoch_hbm,
    out,
    embed_ref, solution_ref, targets_ref, lengths_ref, ids_ref, epoch_ref,
    colb, cola, colt, rowe, rowa, rowt, kst, facc, fitb, fit_x, fit_s, fit_y,
    adjb, acr, wgt, idb, perm, dnt, gtb, cgf, cgx, cgr, cgs, cgd, rgb, rgf, rgs, rg_x, rg_s, rg_y,
    ssem, rsem, lsem,
):
    h, z, c, x, l = place()
    count = [0]
    sent = []

    def send(src, dst, device):
        i = count[0]
        count[0] += 1
        copy = pltpu.make_async_remote_copy(
            src_ref=src, dst_ref=dst, send_sem=ssem.at[i], recv_sem=rsem.at[i],
            device_id=device, device_id_type=MESH,
        )
        copy.start()
        sent.append(copy)
        return copy

    core_peer = at(h, z, 1 - c, x, l)
    far_peer = at(1 - h, z, c, x, 3 - l)
    z_peer = lambda d: at(h, (z + d + 8) % 8, c, x, l)
    plane_peer = lambda dx, dl: at(h, z, c, (x + dx + 4) % 4, (l + dl + 4) % 4)

    barrier = pltpu.get_barrier_semaphore()
    peers = [core_peer, far_peer] + [z_peer(d) for d in (1, -1, 2, -2)]
    peers += [plane_peer(d, 0) for d in (1, 2, 3)] + [plane_peer(0, d) for d in (1, 2, 3)]
    for peer in peers:
        pl.semaphore_signal(barrier, inc=1, device_id=peer, device_id_type=MESH)

    loads = [
        pltpu.make_async_copy(src, dst, lsem.at[i])
        for i, (src, dst) in enumerate([
            (solution_hbm, solution_ref), (epoch_hbm, epoch_ref), (embed_hbm, embed_ref),
            (ids_hbm, ids_ref), (targets_hbm, targets_ref), (lengths_hbm, lengths_ref),
        ])
    ]
    for load in loads:
        load.start()
    for load in loads[:4]:
        load.wait()

    def block(slot):
        return pl.ds(slot * OWN, OWN)

    fitted = jnp.dot(
        solution_ref[...], epoch_ref[...], precision=lax.Precision.HIGHEST, preferred_element_type=F32
    )
    colb[0:OWN, 0:D] = embed_ref[...]
    colb[0:OWN, D : D + E] = fitted.astype(BF16)
    rowe[0:OWN, :] = embed_ref[...]
    ids = ids_ref[...]
    idb[0] = jnp.broadcast_to(jnp.concatenate([ids, ids], axis=1), (8, 128))
    pl.semaphore_wait(barrier, len(peers))

    def slot_of(far, zrel, other):
        return far * 16 + ZSLOT[zrel] * 2 + other

    came = {}

    def forward(far, zrel, steps):
        for step in steps:
            goal = zrel - step
            came[far, ZSLOT[goal]] = send(
                colb.at[block(slot_of(far, zrel, 0)), :], colb.at[block(slot_of(far, goal, 0)), :], z_peer(step)
            )

    def share(far, zrel):
        came[far, ZSLOT[zrel], "core"] = send(
            colb.at[block(slot_of(far, zrel, 0)), :], colb.at[block(slot_of(far, zrel, 1)), :], core_peer
        )

    def arrive(far, zrel):
        came[far, ZSLOT[zrel]].wait_recv()
        share(far, zrel)

    far_copy = send(colb.at[block(0), :], colb.at[block(16), :], far_peer)
    forward(0, 0, (1, -1, 2, -2))
    share(0, 0)

    def gather_rows(ref):
        along_l = [send(ref(0), ref(d), plane_peer(0, -d)) for d in (1, 2, 3)]
        along_x = {}

        def go(e, d):
            along_x[e, d] = send(ref(d), ref(e * 4 + d), plane_peer(-e, 0))

        for e in (1, 3, 2):
            go(e, 0)

        def spread():
            for d, copy in zip((1, 2, 3), along_l):
                copy.wait_recv()
                go(1, d), go(3, d)
            for d in (1, 2, 3):
                go(2, d)

        def finish(e):
            for d in range(4):
                along_x[e, d].wait_recv()

        return spread, finish

    spread_rows, finish_rows = gather_rows(lambda s: rowe.at[block(s), :])

    arrive(0, -1), arrive(0, 1)
    spread_rows()
    arrive(0, -2)
    forward(0, -2, (2, 1))
    arrive(0, 2)
    forward(0, 2, (-1,))
    far_copy.wait_recv()
    forward(1, 0, (-2, 2, -1, 1))
    share(1, 0)
    for e in (1, 2, 3):
        finish_rows(e)
    id_copies = [send(idb.at[0], idb.at[s], plane_peer(-(s // 4), -(s % 4))) for s in range(1, 16)]
    rowe_all = rowe[...]
    rowa[:, 0:D] = (rowe_all.astype(F32) * (1.0 / 64)).astype(BF16)
    rowa[:, D:] = extended(rowe_all, True)

    def columns_in(part):
        for k in range(4 * part, 4 * part + 4):
            came[k // 8, k % 8, "core"].wait_recv()
        cols = slice(part * PART, (part + 1) * PART)
        embed = colb[cols, 0:D]
        cola[cols, 0:D] = embed
        cola[cols, D:] = extended(embed, False)

    def kernel_rows(part, r):
        rows = slice(r * STEP, (r + 1) * STEP)
        cols = slice(part * PART, (part + 1) * PART)
        kern = jnp.exp(lax.dot_general(rowa[rows, :], cola[cols, :], NT, preferred_element_type=F32))
        kst[2 * part, rows, :] = kern[:, 0:STEP]
        kst[2 * part + 1, rows, :] = kern[:, STEP:PART]

    def fit_rows(part, r):
        rows = slice(r * STEP, (r + 1) * STEP)
        total = None if part == 0 else facc[rows, :]
        for i in (2 * part, 2 * part + 1):
            field = colb[i * STEP : (i + 1) * STEP, D : D + E]
            one = jnp.dot(kst[i, rows, :].astype(BF16), field, preferred_element_type=F32)
            total = one if total is None else total + one
        facc[rows, :] = total

    def fit_part(part, done=lambda r: None):
        columns_in(part)
        order = (2, 1, 3, 0)
        kernel_rows(part, order[0])
        for n, r in enumerate(order):
            if n < 3:
                kernel_rows(part, order[n + 1])
            fit_rows(part, r)
            done(r)

    fit_part(0)
    arrive(1, 2)
    forward(1, 2, (-2, -1))
    arrive(1, -2)
    forward(1, -2, (1,))
    arrive(1, -1), arrive(1, 1)
    arrive(0, -3), arrive(0, 3), arrive(0, 4)
    fit_part(2)
    fit_part(1)
    arrive(1, -3), arrive(1, 3), arrive(1, 4)

    def scatter(d, ref, got):
        return {r: send(ref.at[block(4 * d + r), :], got.at[4 * (d - 1) + r], plane_peer(d, 0)) for r in (2, 1, 3, 0)}

    def reduce_rows(copies, mine, got, going, ends):
        last = []
        for r in (2, 1, 3, 0):
            for d in (2, 1, 3):
                copies[d][r].wait_recv()
            rows = block(r)
            mine[rows, :] += sum(got[4 * d + r].astype(F32) for d in range(3))
            if r:
                going[r - 1] = mine[rows, :].astype(BF16)
                last.append(send(going.at[r - 1], ends.at[r - 1], plane_peer(0, r)))
        return last

    passing, below, above = {}, {}, {}

    def put(d, r, slot, step):
        return send(fitb.at[block(4 * d + r), :], fit_x.at[slot], plane_peer(step, 0))

    def leave(d):
        if d == 2:
            rows = slice(d * STEP, (d + 1) * STEP)
            fitb[rows, :] = facc[rows, :].astype(BF16)
            for r in (2, 3, 1, 0):
                passing[r] = put(2, r, 8 + r, 1 if r in (1, 2) else -1)
        if d == 1:
            for r in (3, 0):
                fitb[block(4 + r), :] = facc[block(4 + r), :].astype(BF16)
                below[r] = put(1, r, r, 1)
        if d == 3:
            for r in (2, 1):
                fitb[block(12 + r), :] = facc[block(12 + r), :].astype(BF16)
                above[r] = put(3, r, 4 + r, -1)

    fit_part(3, leave)
    for r in (2, 3, 1, 0):
        passing[r].wait_recv()
        d = 1 if r in (1, 2) else 3
        fitb[block(4 * d + r), :] = (facc[block(4 * d + r), :] + fit_x[8 + r].astype(F32)).astype(BF16)
        if d == 1:
            below[r] = put(1, r, r, 1)
        else:
            above[r] = put(3, r, 4 + r, -1)
    fit_last = []
    for r in (2, 3, 1, 0):
        below[r].wait_recv()
        above[r].wait_recv()
        facc[block(r), :] += fit_x[r].astype(F32) + fit_x[4 + r].astype(F32)
        if r:
            fit_s[r - 1] = facc[block(r), :].astype(BF16)
            fit_last.append(send(fit_s.at[r - 1], fit_y.at[r - 1], plane_peer(0, r)))

    rowt[...] = rowa[...].T[0:TURNED]
    colt[...] = colb[:, 0:D].T
    for copy in id_copies:
        copy.wait_recv()
    lane = lax.broadcasted_iota(I32, (1, 128), 1)

    @pl.loop(0, 8)
    def _(i):
        both = jnp.where(lane < OWN, idb[2 * i, 0:1, :], idb[2 * i + 1, 0:1, :])
        across_x = (((both >> 8) & 3) - x) & 3
        across_l = (((both >> 6) & 3) - l) & 3
        goal = across_x * 256 + across_l * OWN + (both & (OWN - 1))
        seat = lax.broadcasted_iota(I32, (ROWS, 128), 0)
        perm[i // 2, :, pl.ds(pl.multiple_of((i % 2) * 128, 128), 128)] = jnp.where(seat == goal, 1.0, 0.0).astype(BF16)

    for load in loads[4:]:
        load.wait()
    diagonal = lax.broadcasted_iota(I32, (OWN, OWN), 0) == lax.broadcasted_iota(I32, (OWN, OWN), 1)
    spans = jnp.broadcast_to(lengths_ref[...].astype(F32), (OWN, OWN))
    span = jnp.sum(jnp.where(diagonal, spans, 0.0), axis=1, keepdims=True)
    epoch = lax.broadcasted_iota(I32, (OWN, E), 1).astype(F32)

    total = facc[0:OWN, :]
    for copy in fit_last:
        copy.wait_recv()
    total += sum(fit_y[r].astype(F32) for r in range(3))
    adjoint = jnp.where(epoch < span, targets_ref[...].astype(F32) - total, 0.0).astype(BF16)
    adjb[0:OWN, :] = adjoint
    spread_adjoint, finish_adjoint = gather_rows(lambda s: adjb.at[block(s), :])
    spread_adjoint()

    def weigh(i, rows):
        cols = slice(i * STEP, (i + 1) * STEP)
        link = lax.dot_general(adjb[rows, :], colb[cols, D : D + E], NT, preferred_element_type=F32)
        wgt[i, rows, :] = (link * kst[i, rows, :]).astype(BF16)

    def across(i, rows):
        part = jnp.dot(wgt[i, rows, :], cola[i * STEP : (i + 1) * STEP, :], preferred_element_type=F32)
        if i == order[0]:
            acr[rows, :] = part
        else:
            acr[rows, :] += part

    def down(i, rows):
        return jnp.dot(rowt[:, rows], wgt[i, rows, :], preferred_element_type=F32)

    order = (7, 6, 5, 4, 3, 2, 1, 0)

    def rows_arrived(e):
        rows = slice(e * STEP, (e + 1) * STEP)
        weigh(order[0], rows)
        for n, i in enumerate(order):
            if n < 7:
                weigh(order[n + 1], rows)
            across(i, rows)
            part = down(i, rows)
            if e == 0:
                dnt[i] = part
            else:
                dnt[i] += part

    rows_arrived(0)
    finish_adjoint(1)
    rows_arrived(1)
    finish_adjoint(3)
    finish_adjoint(2)

    def finish(i, n):
        total = dnt[i] + down(i, rest)
        gtb[n] = total[0:D] * 64.0 - colt[:, i * STEP : (i + 1) * STEP].astype(F32) * total[D : D + 1]

    def turn(i, n):
        turned = gtb[n].T
        for s in range(2):
            cgf[2 * i + s] = turned[2 * s * OWN : (2 * s + 1) * OWN]
            cgx[2 * i + s] = turned[(2 * s + 1) * OWN : (2 * s + 2) * OWN].astype(BF16)

    def swap(i):
        pair = pl.ds(2 * i, 2)
        swaps[i] = send(cgx.at[pair], cgr.at[pair], core_peer)

    col_copies = []
    swaps = {}

    def add_cores(i):
        swaps[i].wait_recv()
        for k in (2 * i + 1, 2 * i):
            if k == 0:
                continue
            far, zrel = k // 8, ZREL[k % 8]
            cgs[k] = (cgf[k] + cgr[k].astype(F32)).astype(BF16)
            owner = at((h + far) % 2, (z + zrel + 8) % 8, c, x, 3 - l if far else l)
            col_copies.append((k, send(cgs.at[k], cgd.at[k], owner)))

    rest = slice(2 * STEP, ROWS)
    weigh(order[0], rest)
    for n, i in enumerate(order):
        if n < 7:
            weigh(order[n + 1], rest)
        across(i, rest)
        if n < EARLY:
            finish(i, n)
        if 0 < n <= EARLY:
            turn(order[n - 1], n - 1)
            swap(order[n - 1])

    sums = acr[:, D + 3 : D + 4]
    rgb[...] = (acr[:, 0:D] - rowe[...].astype(F32) * sums).astype(BF16)

    def placed(d):
        rows = slice(d * STEP, (d + 1) * STEP)
        return sum(
            jnp.dot(perm[i, rows, :], rgb[i * STEP : (i + 1) * STEP, :], preferred_element_type=F32) for i in range(4)
        )

    row_copies = {}
    for d in (2, 1, 3):
        rgs[d * STEP : (d + 1) * STEP, :] = placed(d).astype(BF16)
        row_copies[d] = scatter(d, rgs, rg_x)
    rgf[...] = placed(0)
    for n in range(EARLY):
        add_cores(order[n])
    for n in range(EARLY, 8):
        finish(order[n], n)
        turn(order[n], n)
        swap(order[n])
    for n in range(EARLY, 8):
        add_cores(order[n])

    row_last = reduce_rows(row_copies, rgf, rg_x, rg_s, rg_y)
    for copy in row_last:
        copy.wait_recv()
    row_total = rgf[0:OWN, :] + sum(rg_y[r].astype(F32) for r in range(3))
    out[0] = row_total * (2.0 / D)

    for k, copy in col_copies:
        copy.wait_recv()
    col_total = cgf[0] + cgr[0].astype(F32)
    for k, copy in col_copies:
        col_total += cgd[k].astype(F32)
    out[1] = col_total * (2.0 / D)
    for copy in sent:
        copy.wait_send()


def per_device(curve_embed, solution, targets, lengths, slot_curve, epoch_kernel):
    vmem = pl.BlockSpec(memory_space=pltpu.VMEM)
    scratch = [
        ((OWN, D), BF16), ((OWN, E), F32), ((OWN, E), BF16), ((1, OWN), I32), ((1, OWN), I32), ((E, E), F32),
        ((COLS, D + E), BF16), ((COLS, 2 * D), BF16), ((D, COLS), BF16), ((ROWS, D), BF16), ((ROWS, 2 * D), BF16),
        ((TURNED, ROWS), BF16), ((COLS // STEP, ROWS, STEP), F32), ((ROWS, E), F32), ((ROWS, E), BF16),
        ((12, OWN, E), BF16), ((3, OWN, E), BF16), ((3, OWN, E), BF16),
        ((ROWS, E), BF16), ((ROWS, 2 * D), F32), ((COLS // STEP, ROWS, STEP), BF16), ((16, 8, 128), I32), ((4, ROWS, STEP), BF16),
        ((COLS // STEP, TURNED, STEP), F32), ((8, D, STEP), F32),
        ((16, OWN, D), F32), ((16, OWN, D), BF16), ((16, OWN, D), BF16), ((16, OWN, D), BF16),
        ((16, OWN, D), BF16), ((ROWS, D), BF16), ((STEP, D), F32), ((ROWS, D), BF16),
        ((12, OWN, D), BF16), ((3, OWN, D), BF16), ((3, OWN, D), BF16),
    ]
    both = pl.pallas_call(
        kernel,
        out_shape=jax.ShapeDtypeStruct((2, OWN, D), F32),
        in_specs=[pl.BlockSpec(memory_space=pl.ANY)] * 6,
        out_specs=vmem,
        scratch_shapes=[pltpu.VMEM(s, t) for s, t in scratch]
        + [pltpu.SemaphoreType.DMA((160,)), pltpu.SemaphoreType.DMA((160,)), pltpu.SemaphoreType.DMA((6,))],
        compiler_params=pltpu.CompilerParams(
            collective_id=0, has_side_effects=True, vmem_limit_bytes=56 * 2**20
        ),
        name="tile",
    )(curve_embed, solution, targets, lengths.reshape(1, OWN), slot_curve.reshape(1, OWN), epoch_kernel)
    return both[0], both[1]


def solution(mesh):
    both = ("row", "col")
    return jax.shard_map(
        per_device,
        mesh=mesh,
        in_specs=(P(both, None), P(both, None), P(both, None), P(both), P(both), P()),
        out_specs=(P(both, None), P(both, None)),
        check_vma=False,
    )
```
